32 devices in a mesh: groups: 2 (over y), slab: 4 (over z), sub: 4 (over x, core).
Axes of the slice: x: 2, y: 2, z: 4, core: 2. Of those that a mesh axis runs over, the one named last changes fastest.
Arguments:
- image: bfloat16 [2, 32, 128, 128], P(None, ('groups', 'slab', 'sub')), parts along dimension 1, may hold values from -6 to 6
- w_in: bfloat16 [9, 32, 2], replicated, may hold values from -2 to 2
- w_down2: bfloat16 [9, 64, 32], replicated, may hold values from -0.5 to 0.5
- w_down3: bfloat16 [9, 128, 64], replicated, may hold values from -0.375 to 0.375
- w_up3: bfloat16 [9, 64, 128], replicated, may hold values from -0.25 to 0.25
- w_up2: bfloat16 [9, 32, 64], replicated, may hold values from -0.375 to 0.375
- w_up1: bfloat16 [9, 32, 32], replicated, may hold values from -0.5 to 0.5
- w_out: bfloat16 [3, 32], replicated, may hold values from -1 to 1
Outputs:
- flows: float32 [4, 32, 128, 128], P(None, ('groups', 'slab', 'sub')), parts along dimension 1
The draws below stay inside these ranges and needn't reach their ends.
There are 2 independent parts, one for each index of `groups`. The reference program is written for one: setup_inputs(seed, part) draws one part's arguments, and reference() takes and returns one part's arrays. A program takes and returns all parts, laid end to end along the dimension named above; an argument that names none is the same for every part. Nothing has to cross between parts.
All inputs are finite; a program needn't handle non-finite values.
Results may differ from the reference program's by a relative error of at most 0.024.
Values may be sent and summed in bfloat16 or wider, within the bound.
A program may use at most 128 MiB of HBM per device.

```python
import jax
import jax.numpy as jnp
from jax import lax

C_IN = 2
C1 = 32
C2 = 64
C3 = 128
SIDE = 128
NZ = 16


def block_scale(rng, dims, cuts, smallest, top_value):
    loudness = 1.0
    for dim, shards_of in cuts:
        heights = jax.random.uniform(jax.random.fold_in(jax.random.fold_in(rng, 6), dim), (shards_of,), jnp.float32, smallest / len(cuts), top_value / len(cuts))
        loudness = loudness * jnp.repeat(jnp.exp(heights), dims[dim] // shards_of).reshape((-1,) + (1,) * (len(dims) - 1 - dim))
    return loudness


def centred(rng, shape, deviation, reach, shards=(), held_as=jnp.bfloat16):
    drawn = deviation * jax.random.normal(rng, shape, jnp.float32)
    if shards:
        drawn = drawn * block_scale(rng, shape, shards, -0.22, 0.18)
    return jnp.clip(drawn, -reach, reach).astype(held_as)


def setup_inputs(seed: int = 0, part: int = 0) -> dict:
    splits = jax.random.split(jax.random.key(seed), 9)
    part_splits = jax.random.split(jax.random.fold_in(splits[8], part), 9)
    return {
        "image": centred(part_splits[0], (C_IN, NZ, SIDE, SIDE), 1.0, 6.0, ((1, 16),)),
        "w_in": centred(splits[1], (9, C1, C_IN), (9 * C_IN // 2) ** -0.5, 2.0),
        "w_down2": centred(splits[2], (9, C2, C1), (9 * C1 // 2) ** -0.5, 0.5),
        "w_down3": centred(splits[3], (9, C3, C2), (9 * C2 // 2) ** -0.5, 0.375),
        "w_up3": centred(splits[4], (9, C2, C3), (9 * C3 // 2) ** -0.5, 0.25),
        "w_up2": centred(splits[5], (9, C1, C2), (9 * C2 // 2) ** -0.5, 0.375),
        "w_up1": centred(splits[6], (9, C1, C1), (9 * C1 // 2) ** -0.5, 0.5),
        "w_out": centred(splits[7], (3, C1), C1 ** -0.5, 1.0),
    }


def conv_three(values, kernel):
    height, span = values.shape[2], values.shape[3]
    padded = jnp.pad(values.astype(jnp.float32), ((0, 0), (0, 0), (1, 1), (1, 1)))
    summed = jnp.zeros((values.shape[0], kernel.shape[1], height, span), jnp.float32)
    for kernel_tap in range(9):
        down_off = kernel_tap // 3
        right_off = kernel_tap % 3
        window = padded[:, :, down_off:down_off + height, right_off:right_off + span]
        summed = summed + jnp.einsum("oc,bchw->bohw", kernel[kernel_tap].astype(jnp.float32), window)
    return summed


def relu_round(values):
    return jnp.maximum(values, 0.0).astype(jnp.bfloat16)


def pool_half(values):
    count, chan_num, height, span = values.shape
    blocks = values.astype(jnp.float32).reshape(count, chan_num, height // 2, 2, span // 2, 2)
    return jnp.mean(blocks, axis=(3, 5)).astype(jnp.bfloat16)


def upsample(values):
    return jnp.repeat(jnp.repeat(values, 2, axis=2), 2, axis=3)


def run_unet(slices, weights):
    w_in, w_down2, w_down3, w_up3, w_up2, w_up1, w_out = weights
    level_one = relu_round(conv_three(slices, w_in))
    level_two = relu_round(conv_three(pool_half(level_one), w_down2))
    level_three = relu_round(conv_three(pool_half(level_two), w_down3))
    decoded_three = relu_round(conv_three(level_three, w_up3))
    skip_two = (upsample(decoded_three).astype(jnp.float32) + level_two.astype(jnp.float32)).astype(jnp.bfloat16)
    decoded_two = relu_round(conv_three(skip_two, w_up2))
    skip_one = (upsample(decoded_two).astype(jnp.float32) + level_one.astype(jnp.float32)).astype(jnp.bfloat16)
    decoded_one = relu_round(conv_three(skip_one, w_up1))
    return jnp.einsum("oc,bchw->bohw", w_out.astype(jnp.float32), decoded_one.astype(jnp.float32))


def run_blocks(slices, weights):
    count = slices.shape[0]
    grouped = slices.reshape((count // 8, 8) + slices.shape[1:])
    result = lax.map(lambda block_in: run_unet(block_in, weights), grouped)
    return result.reshape((count,) + result.shape[2:])


def reference(image, w_in, w_down2, w_down3, w_up3, w_up2, w_up1, w_out):
    weights = (w_in, w_down2, w_down3, w_up3, w_up2, w_up1, w_out)
    flows_xy = jnp.transpose(run_blocks(jnp.transpose(image, (1, 0, 2, 3)), weights), (1, 0, 2, 3))
    flows_xz = jnp.transpose(run_blocks(jnp.transpose(image, (2, 0, 1, 3)), weights), (1, 2, 0, 3))
    flows_yz = jnp.transpose(run_blocks(jnp.transpose(image, (3, 0, 1, 2)), weights), (1, 2, 3, 0))
    flow_z = (flows_xz[0] + flows_yz[0]) * 0.5
    flow_y = (flows_xy[0] + flows_yz[1]) * 0.5
    flow_x = (flows_xy[1] + flows_xz[1]) * 0.5
    probability = (flows_xy[2] + flows_xz[2] + flows_yz[2]) / 3.0
    return jnp.stack([flow_z, flow_y, flow_x, probability], axis=0)
```

```python
import functools

import jax
import jax.numpy as jnp
from jax import lax
from jax.experimental import pallas as pl
from jax.experimental.pallas import tpu as pltpu
from jax.sharding import PartitionSpec as P

F32, BF16 = jnp.float32, jnp.bfloat16
AXES = ("slab", "sub")
UNITS = 16
OFF = 4
SLOTS = (0, 2, 1, 3)


def lanes(shape):
    return lax.broadcasted_iota(jnp.int32, shape, len(shape) - 1)


def turn(values, shift):
    shift = shift % 128
    return pltpu.roll(values, shift, values.ndim - 1) if shift else values


def build_band(tap, chan, made, cells, slots, scale, band_ref):
    shape = (chan, 128)
    slot_of_lane = lanes(shape) // made
    tiled = [jnp.concatenate([tap(n) * scale] * (128 // made), axis=1) for n in range(9)]
    for number, (a, b) in enumerate(cells):
        for r in range(2):
            total = jnp.zeros(shape, F32)
            for slot, c in enumerate(slots):
                down, right = a - r + 1, b - c + 1
                if 0 <= down < 3 and 0 <= right < 3:
                    value = tiled[3 * down + right]
                    total = value if len(slots) == 1 else jnp.where(slot_of_lane == slot, value, total)
            band_ref[number * chan : (number + 1) * chan, 128 * r : 128 * r + 128] = total.astype(BF16)


def build_in(tap, band_ref):
    shape = (128, 128)
    row = lax.broadcasted_iota(jnp.int32, shape, 0)
    slot = lanes(shape) // 32
    col = slot % 2 * 2 + slot // 2
    chan, down, place = row // 16 % 2, row // 32, row % 16
    tiled = [jnp.concatenate([tap(n)] * 4, axis=1) for n in range(9)]
    for q in range(2):
        right = place - OFF - 4 * q - col + 1
        ok = (right >= 0) & (right < 3)
        for r in range(2):
            code = jnp.where(ok, ((down - r) * 3 + right) * 2 + chan, -1)
            total = jnp.zeros(shape, F32)
            for number in range(9):
                for k in range(2):
                    total = jnp.where(code == number * 2 + k, tiled[number][k : k + 1, :], total)
            start = 256 * q + 128 * r
            band_ref[:, start : start + 128] = total.astype(BF16)


def build_out(weight, band_ref):
    flipped = weight.T
    shape = (32, 128)
    lane = lanes(shape)
    for q in range(8):
        for r in range(2):
            for slot, c in enumerate(SLOTS):
                start = 256 * q + 128 * r + 32 * slot
                for half in range(2):
                    total = jnp.zeros(shape, F32)
                    for out in range(3):
                        piece = 2 * out + r
                        if piece // 4 == half:
                            here = lane == 32 * (piece % 4) + 4 * q + c
                            total = jnp.where(here, flipped[:, out : out + 1], total)
                    band_ref[start : start + 32, 128 * half : 128 * half + 128] = total.astype(BF16)


CELLS_DOWN2 = [(a, b) for a in range(-1, 3) for b in (0, 1, 2, -1)]
CELLS_DOWN3 = [(a, b) for a in range(-1, 3) for b in (0, 1)] + [(a, -1) for a in range(-1, 3)]
CELLS_UP3 = [(a, b) for b in range(-1, 3) for a in range(-1, 3)]
CELLS_UP2 = [(a, b) for a in range(-1, 3) for b in (0, 1, 2, 3, 4, -1)]
CELLS_UP1 = [(a, b) for a in range(-1, 3) for b in SLOTS] + [
    (-1, 4), (0, -1), (0, 4), (-1, -1), (1, 4), (2, -1), (2, 4), (1, -1)
]


def build_all(weights, bands):
    w_in, w_down2, w_down3, w_up3, w_up2, w_up1, w_out = weights
    build_in(lambda n: w_in[n].astype(F32), bands[0])
    build_band(lambda n: w_down2[n].astype(F32), 32, 64, CELLS_DOWN2, (0, 1), 0.25, bands[1])
    build_band(lambda n: w_down3[n].astype(F32), 64, 128, CELLS_DOWN3, (0,), 0.25, bands[2])
    build_band(lambda n: w_up3[n].astype(F32).T, 128, 64, CELLS_UP3, (0, 1), 1.0, bands[3])
    build_band(lambda n: w_up2[n].astype(F32).T, 64, 32, CELLS_UP2, (0, 1, 2, 3), 1.0, bands[4])
    build_band(lambda n: w_up1[n].astype(F32).T, 32, 32, CELLS_UP1, SLOTS, 1.0, bands[5])
    build_out(w_out[...].astype(F32), bands[6])


BAND_SCRATCH = [
    pltpu.VMEM((128, 512), BF16),
    pltpu.VMEM((512, 256), BF16),
    pltpu.VMEM((768, 256), BF16),
    pltpu.VMEM((2048, 256), BF16),
    pltpu.VMEM((1536, 256), BF16),
    pltpu.VMEM((768, 256), BF16),
    pltpu.VMEM((2048, 256), BF16),
]


def beside(values, step):
    zero = jnp.zeros((1,) + values.shape[1:], values.dtype)
    if step > 0:
        return jnp.concatenate([values[1:], zero], axis=0)
    return jnp.concatenate([zero, values[:-1]], axis=0)


def strip_above(values, parts):
    values = values.astype(F32)
    if parts == UNITS:
        return jnp.zeros_like(values)
    axis = values.ndim - 2
    unit = lax.broadcasted_iota(jnp.int32, values.shape, axis)
    return jnp.where(unit < parts, 0.0, pltpu.roll(values, parts, axis))


def strip_below(values, parts):
    values = values.astype(F32)
    if parts == UNITS:
        return jnp.zeros_like(values)
    axis = values.ndim - 2
    unit = lax.broadcasted_iota(jnp.int32, values.shape, axis)
    return jnp.where(unit >= UNITS - parts, 0.0, pltpu.roll(values, UNITS - parts, axis))


def matmul(pieces, band_ref):
    rows = jnp.concatenate(pieces, axis=-1)
    lead = rows.shape[:-1]
    flat = rows.reshape(lead[0] * lead[1], rows.shape[-1])
    total = jnp.dot(flat, band_ref[...], preferred_element_type=F32)
    return total.reshape(lead + (total.shape[-1],))


def relu(values):
    return jnp.maximum(values, 0.0)


def unit_scratch(height, wide):
    pairs, half, quarter = height // 2, height // 4, height // 8
    blocks = wide // 4
    return [
        pltpu.VMEM((2, height + 2, UNITS, wide), F32),
        pltpu.VMEM((pairs, blocks // 2, UNITS, 128), BF16),
        pltpu.VMEM((pairs, blocks // 2, UNITS, 512), BF16),
        pltpu.VMEM((pairs + 2, blocks, UNITS, 128), BF16),
        pltpu.VMEM((half, blocks, UNITS, 256), BF16),
        pltpu.VMEM((half + 2, blocks, UNITS, 128), BF16),
        pltpu.VMEM((quarter + 1, blocks, UNITS, 128), BF16),
        pltpu.VMEM((quarter + 2, blocks + 2, UNITS, 256), BF16),
        pltpu.VMEM((half + 2, blocks, UNITS, 256), BF16),
        pltpu.VMEM((half + 2, blocks // 2, UNITS, 256), BF16),
        pltpu.VMEM((pairs + 2, blocks, UNITS, 256), BF16),
        pltpu.VMEM((pairs + 1, blocks, UNITS, 128), BF16),
        pltpu.VMEM((pairs, blocks, UNITS, 256), BF16),
    ]


class Net:
    def __init__(self, height, wide, parts, bands, scratch):
        self.height, self.wide, self.parts = height, wide, parts
        self.bands = bands
        (self.x, self.win, self.a1, self.q1, self.a2, self.u, self.t, self.a3) = scratch[:8]
        (self.s2, self.h2, self.s1, self.h1, self.c1) = scratch[8:]
        self.pairs, self.half, self.quarter = height // 2, height // 4, height // 8
        self.blocks = wide // 4

    def fill(self, load):
        x, height = self.x, self.height
        for chan in range(2):
            for h in range(height):
                x[chan, h + 1] = load(chan, h)
            x[chan, 0] = strip_above(x[chan, height], self.parts)
            x[chan, height + 1] = strip_below(x[chan, 1], self.parts)
        lane = lanes((UNITS, 128))
        count = self.wide // 8
        for t in range(self.pairs):
            pieces = [turn(x[p % 2, 2 * t + p // 2], 16 * p) for p in range(8)]
            for parity in range(2):
                group = (lane + OFF - 8 * parity + 128) // 16
                picked = pieces
                for bit in range(3):
                    take = group // (1 << bit) % 2 == 1
                    picked = [
                        jnp.where(take, picked[(i + (1 << bit)) % 8], picked[i]) for i in range(8)
                    ]
                for k in range(parity, count, 2):
                    window = turn(picked[-(k // 2) % 8], OFF - 8 * k)
                    if k == 0:
                        window = jnp.where(lane % 16 < OFF, 0.0, window)
                    if k == count - 1:
                        window = jnp.where(lane % 16 >= OFF + 8, 0.0, window)
                    self.win[t, k] = window.astype(BF16)

    def level1(self):
        lane = lanes((self.blocks, UNITS, 128))
        for t in range(self.pairs):
            values = relu(matmul([self.win[t]], self.bands[0]))
            self.a1[t] = values.astype(BF16)
            sums = [values[..., s : s + 128] + values[..., s + 128 : s + 256] for s in (0, 256)]
            both = jnp.concatenate([y[:, None] for y in sums], axis=1)
            both = both.reshape(self.blocks, UNITS, 128)
            both = both + turn(both, 64)
            side = jnp.where(lane < 96, beside(both, 1), beside(both, -1))
            self.q1[t + 1] = jnp.where(lane < 64, both, side).astype(BF16)
        self.q1[0] = strip_above(self.q1[self.pairs], self.parts).astype(BF16)
        self.q1[self.pairs + 1] = strip_below(self.q1[1], self.parts).astype(BF16)

    def level2(self):
        low = lanes((self.blocks, UNITS, 128)) < 64
        for t in range(self.half):
            values = relu(matmul([self.q1[2 * t + a] for a in range(4)], self.bands[1]))
            self.a2[t] = values.astype(BF16)
            cell = values[..., :128] + values[..., 128:]
            cell = cell + turn(cell, 64)
            self.u[t + 1] = jnp.where(low, cell, beside(cell, 1)).astype(BF16)
            left = beside(cell, -1).astype(BF16)
            if t % 2 == 0:
                self.t[t // 2, :, :, 64:] = left[..., 64:]
            else:
                self.t[(t + 1) // 2, :, :, :64] = left[..., :64]
        self.u[0] = strip_above(self.u[self.half], self.parts).astype(BF16)
        self.u[self.half + 1] = strip_below(self.u[1], self.parts).astype(BF16)
        last = self.quarter
        above = strip_above(self.t[last], self.parts).astype(BF16)
        below = strip_below(self.t[0], self.parts).astype(BF16)
        self.t[0, :, :, :64] = above[..., :64]
        self.t[last, :, :, 64:] = below[..., 64:]

    def level3(self):
        for t in range(self.quarter):
            pieces = [self.u[2 * t + a] for a in range(4)] + [self.t[t], self.t[t + 1]]
            self.a3[t + 1, 1 : self.blocks + 1] = relu(matmul(pieces, self.bands[2])).astype(BF16)
        last = self.quarter
        zero = jnp.zeros((last + 2, UNITS, 256), BF16)
        self.a3[:, 0] = zero
        self.a3[:, self.blocks + 1] = zero
        self.a3[0, :, :, 128:] = strip_above(self.a3[last, :, :, 128:], self.parts).astype(BF16)
        self.a3[last + 1, :, :, :128] = strip_below(self.a3[1, :, :, :128], self.parts).astype(BF16)

    def level3_up(self):
        count = self.blocks // 2
        low = lanes((count, UNITS, 128)) < 64
        for t in range(self.quarter):
            pieces = []
            for b in range(4):

                def column(row, start):
                    values = self.a3[row, 2 * (b // 2) : 2 * (b // 2) + self.blocks, :, start : start + 128]
                    return values.reshape(count, 2, UNITS, 128)[:, b % 2]

                pieces += [column(t, 128), column(t + 1, 0), column(t + 1, 128), column(t + 2, 0)]
            values = relu(matmul(pieces, self.bands[3]))
            for r in range(2):
                piece = values[..., 128 * r : 128 * r + 128]
                other = turn(piece, 64)
                cells = [jnp.where(low, piece, other), jnp.where(low, other, piece)]
                both = jnp.concatenate([cell[:, None] for cell in cells], axis=1)
                both = both.reshape(self.blocks, UNITS, 128)
                row = 2 * t + r
                for part in range(2):
                    span = slice(128 * part, 128 * part + 128)
                    skip = both + self.a2[row, :, :, span].astype(F32)
                    self.s2[row + 1, :, :, span] = skip.astype(BF16)
                    pairs = skip.reshape(count, 2, UNITS, 128)
                    halo = jnp.where(low, beside(pairs[:, 0], 1), beside(pairs[:, 1], -1))
                    self.h2[row + 1, :, :, span] = halo.astype(BF16)
        last = self.half
        for ref in (self.s2, self.h2):
            ref[0, :, :, 128:] = strip_above(ref[last, :, :, 128:], self.parts).astype(BF16)
            ref[last + 1, :, :, :128] = strip_below(ref[1, :, :, :128], self.parts).astype(BF16)

    def halo1(self, t, above, below):
        slot = lanes((self.blocks, UNITS, 128)) // 32
        mixed = jnp.where((slot == 0) | (slot == 3), above, turn(below, 64))
        halo = jnp.where(slot % 2 == 0, beside(mixed, 1), beside(mixed, -1))
        self.h1[t] = halo.astype(BF16)

    def level2_up(self):
        count = self.blocks // 2
        low = lanes((count, UNITS, 128)) < 64
        for t in range(self.half):
            pieces = []
            for row, start in ((t, 128), (t + 1, 0), (t + 1, 128), (t + 2, 0)):
                values = self.s2[row, :, :, start : start + 128].reshape(count, 2, UNITS, 128)
                pieces += [values[:, 0], values[:, 1], self.h2[row, :, :, start : start + 128]]
            values = relu(matmul(pieces, self.bands[4]))
            below = None
            for r in range(2):
                piece = values[..., 128 * r : 128 * r + 128]
                other = turn(piece, 64)
                cells = [jnp.where(low, piece, other), jnp.where(low, other, piece)]
                both = jnp.concatenate([cell[:, None] for cell in cells], axis=1)
                both = both.reshape(self.blocks, UNITS, 128)
                row = 2 * t + r
                skips = []
                for part in range(2):
                    parts = [
                        self.a1[row, :, :, 256 * q + 128 * part : 256 * q + 128 * part + 128][:, None]
                        for q in range(2)
                    ]
                    skip = jnp.concatenate(parts, axis=1).reshape(self.blocks, UNITS, 128)
                    skips.append(both + skip.astype(F32))
                    self.s1[row + 1, :, :, 128 * part : 128 * part + 128] = skips[part].astype(BF16)
                if r == 0 and t > 0:
                    below = self.s1[row, :, :, 128:].astype(F32)
                if row > 0:
                    self.halo1(row, below, skips[0])
                below = skips[1]
        last = self.pairs
        above = strip_above(self.s1[last, :, :, 128:], self.parts)
        self.s1[0, :, :, 128:] = above.astype(BF16)
        self.halo1(0, above, self.s1[1, :, :, :128].astype(F32))
        below = strip_below(self.s1[1, :, :, :128], self.parts)
        self.s1[last + 1, :, :, :128] = below.astype(BF16)
        self.halo1(last, self.s1[last, :, :, 128:].astype(F32), below)

    def level1_up(self, begin, end):
        s1, h1 = self.s1, self.h1
        for t in range(begin, end):
            pieces = [s1[t, :, :, 128:], s1[t + 1], s1[t + 2, :, :, :128], h1[t], h1[t + 1]]
            self.c1[t] = relu(matmul(pieces, self.bands[5])).astype(BF16)

    def last(self, begin, end, emit):
        count = self.blocks // 8
        rows = self.c1[begin:end].reshape((end - begin) * count, 8, UNITS, 256)
        values = matmul([rows[:, q] for q in range(8)], self.bands[6])
        values = values.reshape(end - begin, count, UNITS, 256)
        group = lanes((UNITS, 128)) // 32
        for t in range(begin, end):
            for half in range(2):
                span = slice(128 * half, 128 * half + 128)
                picked = [turn(values[t - begin, k, :, span], 32 * k) for k in range(4)]
                for bit in range(2):
                    take = group // (1 << bit) % 2 == 1
                    picked = [
                        jnp.where(take, picked[(i + (1 << bit)) % 4], picked[i]) for i in range(4)
                    ]
                for p in range(4 - 2 * half):
                    piece = 4 * half + p
                    emit(piece // 2, 2 * t + piece % 2, turn(picked[-p % 4], -32 * p))


def peer_id(index, inner):
    return {"slab": index // inner, "sub": lax.rem(index, inner)}


FLAT, CROSS = 13, 13


def window_kernel(peers, inner, image_ref, *refs):
    given, out_ref, bands = refs[:7], refs[7], refs[8:15]
    flat_scratch, cross_scratch = refs[15:28], refs[28:41]
    send, recv, flat, back_send, back, out_sem, in_sem, back_out_sem, back_in_sem = refs[41:50]
    plane_ref, plane, weights, local_sem = refs[50], refs[51], refs[52:59], refs[59]
    copies = [pltpu.make_async_copy(image_ref.at[:, 0], plane_ref, local_sem.at[0])]
    for number in range(7):
        copies.append(
            pltpu.make_async_copy(given[number], weights[number], local_sem.at[1 + number])
        )
    for copy in copies:
        copy.start()
    extent = plane_ref.shape[1]
    cut = extent // peers
    parts = 2 * cut
    strips = UNITS // parts
    deep = peers // strips
    tall = extent // UNITS
    me = lax.axis_index("slab") * inner + lax.axis_index("sub")

    barrier = pltpu.get_barrier_semaphore()

    def greet(k, carry):
        pl.semaphore_signal(
            barrier,
            inc=1,
            device_id=peer_id(lax.rem(me + k, peers), inner),
            device_id_type=pl.DeviceIdType.MESH,
        )
        return carry

    lax.fori_loop(1, peers, greet, 0)
    copies[0].wait()
    for chan in range(2):
        values = plane_ref[chan].astype(F32)
        plane[chan] = values
        runs = [values.reshape(peers, cut, extent), values.T.reshape(peers, cut, extent)]
        send[:, chan] = jnp.concatenate(runs, axis=1).astype(send.dtype)
    recv[pl.ds(me, 1)] = send[pl.ds(me, 1)]
    for copy in copies[1:]:
        copy.wait()
    build_all(weights, bands)
    pl.semaphore_wait(barrier, peers - 1)

    def input_copy(k):
        peer = lax.rem(me + k, peers)
        return pltpu.make_async_remote_copy(
            src_ref=send.at[peer],
            dst_ref=recv.at[me],
            send_sem=out_sem.at[k],
            recv_sem=in_sem.at[k],
            device_id=peer_id(peer, inner),
            device_id_type=pl.DeviceIdType.MESH,
        )

    def result_copy(k):
        peer = lax.rem(me + k, peers)
        return pltpu.make_async_remote_copy(
            src_ref=back_send.at[peer],
            dst_ref=back.at[me],
            send_sem=back_out_sem.at[k],
            recv_sem=back_in_sem.at[k],
            device_id=peer_id(peer, inner),
            device_id_type=pl.DeviceIdType.MESH,
        )

    def start(k, carry):
        input_copy(k).start()
        return carry

    def finish(k, carry):
        input_copy(k).wait()
        return carry

    def start_back(k, carry):
        result_copy(k).start()
        return carry

    def settle(k, carry):
        result_copy(k).wait()
        return carry

    lax.fori_loop(1, peers, start, 0)

    xy = Net(tall, extent, 1, bands, flat_scratch)
    xy.fill(lambda chan, h: plane[chan, pl.ds(h, UNITS, stride=tall), :])
    xy.level1()
    xy.level2()
    xy.level3()
    xy.level3_up()

    lax.fori_loop(1, peers, finish, 0)

    cross = Net(deep, extent, parts, bands, cross_scratch)

    def load_cross(chan, h):
        if strips == 1:
            return recv[h, chan].astype(F32)
        return recv[pl.ds(h, strips, stride=deep), chan].astype(F32).reshape(UNITS, extent)

    def emit_cross(out, h, values):
        if strips == 1:
            back_send[h, out] = values.astype(back_send.dtype)
        else:
            for strip in range(strips):
                piece = values[strip * parts : (strip + 1) * parts]
                back_send[h + strip * deep, out] = piece.astype(back_send.dtype)

    cross.fill(load_cross)
    cross.level1()
    cross.level2()
    cross.level3()
    cross.level3_up()
    cross.level2_up()
    cross.level1_up(0, cross.pairs)
    cross.last(0, cross.pairs, emit_cross)
    back[pl.ds(me, 1)] = back_send[pl.ds(me, 1)]
    lax.fori_loop(1, peers, start_back, 0)

    def emit_flat(out, h, values):
        flat[out, pl.ds(h, UNITS, stride=tall), :] = values

    xy.level2_up()
    xy.level1_up(0, xy.pairs)
    xy.last(0, xy.pairs, emit_flat)

    lax.fori_loop(1, peers, settle, 0)

    def result(run, out):
        values = back[:, out].astype(F32)[:, run * cut : (run + 1) * cut].reshape(extent, extent)
        return values.T if run == 1 else values

    out_ref[0] = (result(0, 0) + result(1, 0)) * 0.5
    out_ref[1] = (flat[0] + result(1, 1)) * 0.5
    out_ref[2] = (flat[1] + result(0, 1)) * 0.5
    out_ref[3] = (flat[2] + result(0, 2) + result(1, 2)) / 3.0


def shards(image, *weights):
    chan, _, extent, _ = image.shape
    peers = lax.axis_size(AXES)
    cut = extent // peers
    parts = 2 * cut
    link = BF16 if parts % UNITS == 0 else F32
    weights = [jnp.swapaxes(weight, 1, 2) for weight in weights[:3]] + list(weights[3:])
    sems = [pltpu.SemaphoreType.DMA((peers,))] * 4
    flows = pl.pallas_call(
        functools.partial(window_kernel, peers, lax.axis_size("sub")),
        out_shape=jax.ShapeDtypeStruct((4, extent, extent), F32),
        in_specs=[pl.BlockSpec(memory_space=pltpu.HBM)] * 8,
        out_specs=pl.BlockSpec(memory_space=pltpu.VMEM),
        scratch_shapes=BAND_SCRATCH
        + unit_scratch(extent // UNITS, extent)
        + unit_scratch(peers * parts // UNITS, extent)
        + [
            pltpu.VMEM((peers, chan, parts, extent), link),
            pltpu.VMEM((peers, chan, parts, extent), link),
            pltpu.VMEM((3, extent, extent), F32),
            pltpu.VMEM((peers, 3, parts, extent), link),
            pltpu.VMEM((peers, 3, parts, extent), link),
        ]
        + sems
        + [pltpu.VMEM((chan, extent, extent), BF16), pltpu.VMEM((chan, extent, extent), F32)]
        + [pltpu.VMEM(weight.shape, BF16) for weight in weights]
        + [pltpu.SemaphoreType.DMA((8,))],
        compiler_params=pltpu.CompilerParams(
            vmem_limit_bytes=50 << 20, collective_id=0, has_side_effects=True
        ),
    )(image, *weights)
    return flows[:, None]


def solution(mesh):
    split = P(None, ("groups", "slab", "sub"), None, None)
    return jax.shard_map(
        shards,
        mesh=mesh,
        in_specs=(split,) + (P(),) * 7,
        out_specs=split,
        check_vma=False,
    )
```

```python
import functools

import jax
import jax.numpy as jnp
from jax import lax
from jax.experimental import pallas as pl
from jax.experimental.pallas import tpu as pltpu
from jax.sharding import PartitionSpec as P

F32, BF16 = jnp.float32, jnp.bfloat16
AXES = ("slab", "sub")
UNITS = 16
OFF = 4
SLOTS = (0, 2, 1, 3)


def lanes(shape):
    return lax.broadcasted_iota(jnp.int32, shape, len(shape) - 1)


def turn(values, shift):
    shift = shift % 128
    return pltpu.roll(values, shift, values.ndim - 1) if shift else values


def build_band(tap, chan, made, cells, slots, scale, band_ref):
    shape = (chan, 128)
    slot_of_lane = lanes(shape) // made
    tiled = [jnp.concatenate([tap(n) * scale] * (128 // made), axis=1) for n in range(9)]
    for number, (a, b) in enumerate(cells):
        for r in range(2):
            total = jnp.zeros(shape, F32)
            for slot, c in enumerate(slots):
                down, right = a - r + 1, b - c + 1
                if 0 <= down < 3 and 0 <= right < 3:
                    value = tiled[3 * down + right]
                    total = value if len(slots) == 1 else jnp.where(slot_of_lane == slot, value, total)
            band_ref[number * chan : (number + 1) * chan, 128 * r : 128 * r + 128] = total.astype(BF16)


def build_in(tap, band_ref):
    shape = (128, 128)
    row = lax.broadcasted_iota(jnp.int32, shape, 0)
    slot = lanes(shape) // 32
    col = slot % 2 * 2 + slot // 2
    chan, down, place = row // 16 % 2, row // 32, row % 16
    tiled = [jnp.concatenate([tap(n)] * 4, axis=1) for n in range(9)]
    for q in range(2):
        right = place - OFF - 4 * q - col + 1
        ok = (right >= 0) & (right < 3)
        for r in range(2):
            code = jnp.where(ok, ((down - r) * 3 + right) * 2 + chan, -1)
            total = jnp.zeros(shape, F32)
            for number in range(9):
                for k in range(2):
                    total = jnp.where(code == number * 2 + k, tiled[number][k : k + 1, :], total)
            start = 256 * q + 128 * r
            band_ref[:, start : start + 128] = total.astype(BF16)


def build_out(weight, band_ref):
    flipped = weight.T
    shape = (32, 128)
    lane = lanes(shape)
    for q in range(8):
        for r in range(2):
            for slot, c in enumerate(SLOTS):
                start = 256 * q + 128 * r + 32 * slot
                for half in range(2):
                    total = jnp.zeros(shape, F32)
                    for out in range(3):
                        piece = 2 * out + r
                        if piece // 4 == half:
                            here = lane == 32 * (piece % 4) + 4 * q + c
                            total = jnp.where(here, flipped[:, out : out + 1], total)
                    band_ref[start : start + 32, 128 * half : 128 * half + 128] = total.astype(BF16)


CELLS_DOWN2 = [(a, b) for a in range(-1, 3) for b in (0, 1, 2, -1)]
CELLS_DOWN3 = [(a, b) for a in range(-1, 3) for b in (0, 1)] + [(a, -1) for a in range(-1, 3)]
CELLS_UP3 = [(a, b) for b in range(-1, 3) for a in range(-1, 3)]
CELLS_UP2 = [(a, b) for a in range(-1, 3) for b in (0, 1, 2, 3, 4, -1)]
CELLS_UP1 = [(a, b) for a in range(-1, 3) for b in SLOTS] + [
    (-1, 4), (0, -1), (0, 4), (-1, -1), (1, 4), (2, -1), (2, 4), (1, -1)
]


def build_all(weights, bands):
    w_in, w_down2, w_down3, w_up3, w_up2, w_up1, w_out = weights
    build_in(lambda n: w_in[n].astype(F32), bands[0])
    build_band(lambda n: w_down2[n].astype(F32), 32, 64, CELLS_DOWN2, (0, 1), 0.25, bands[1])
    build_band(lambda n: w_down3[n].astype(F32), 64, 128, CELLS_DOWN3, (0,), 0.25, bands[2])
    build_band(lambda n: w_up3[n].astype(F32).T, 128, 64, CELLS_UP3, (0, 1), 1.0, bands[3])
    build_band(lambda n: w_up2[n].astype(F32).T, 64, 32, CELLS_UP2, (0, 1, 2, 3), 1.0, bands[4])
    build_band(lambda n: w_up1[n].astype(F32).T, 32, 32, CELLS_UP1, SLOTS, 1.0, bands[5])
    build_out(w_out[...].astype(F32), bands[6])


BAND_SCRATCH = [
    pltpu.VMEM((128, 512), BF16),
    pltpu.VMEM((512, 256), BF16),
    pltpu.VMEM((768, 256), BF16),
    pltpu.VMEM((2048, 256), BF16),
    pltpu.VMEM((1536, 256), BF16),
    pltpu.VMEM((768, 256), BF16),
    pltpu.VMEM((2048, 256), BF16),
]


def beside(values, step):
    zero = jnp.zeros((1,) + values.shape[1:], values.dtype)
    if step > 0:
        return jnp.concatenate([values[1:], zero], axis=0)
    return jnp.concatenate([zero, values[:-1]], axis=0)


def strip_above(values, parts):
    values = values.astype(F32)
    if parts == UNITS:
        return jnp.zeros_like(values)
    axis = values.ndim - 2
    unit = lax.broadcasted_iota(jnp.int32, values.shape, axis)
    return jnp.where(unit < parts, 0.0, pltpu.roll(values, parts, axis))


def strip_below(values, parts):
    values = values.astype(F32)
    if parts == UNITS:
        return jnp.zeros_like(values)
    axis = values.ndim - 2
    unit = lax.broadcasted_iota(jnp.int32, values.shape, axis)
    return jnp.where(unit >= UNITS - parts, 0.0, pltpu.roll(values, UNITS - parts, axis))


def matmul(pieces, band_ref):
    rows = jnp.concatenate(pieces, axis=-1)
    lead = rows.shape[:-1]
    flat = rows.reshape(lead[0] * lead[1], rows.shape[-1])
    total = jnp.dot(flat, band_ref[...], preferred_element_type=F32)
    return total.reshape(lead + (total.shape[-1],))


def relu(values):
    return jnp.maximum(values, 0.0)


def unit_scratch(height, wide):
    pairs, half, quarter = height // 2, height // 4, height // 8
    blocks = wide // 4
    return [
        pltpu.VMEM((2, height + 2, UNITS, wide), F32),
        pltpu.VMEM((pairs, blocks // 2, UNITS, 128), BF16),
        pltpu.VMEM((pairs, blocks // 2, UNITS, 512), BF16),
        pltpu.VMEM((pairs + 2, blocks, UNITS, 128), BF16),
        pltpu.VMEM((half, blocks, UNITS, 256), BF16),
        pltpu.VMEM((half + 2, blocks, UNITS, 128), BF16),
        pltpu.VMEM((quarter + 1, blocks, UNITS, 128), BF16),
        pltpu.VMEM((quarter + 2, blocks + 2, UNITS, 256), BF16),
        pltpu.VMEM((half + 2, blocks, UNITS, 256), BF16),
        pltpu.VMEM((half + 2, blocks // 2, UNITS, 256), BF16),
        pltpu.VMEM((pairs + 2, blocks, UNITS, 256), BF16),
        pltpu.VMEM((pairs + 1, blocks, UNITS, 128), BF16),
        pltpu.VMEM((pairs, blocks, UNITS, 256), BF16),
    ]


class Net:
    def __init__(self, height, wide, parts, bands, scratch):
        self.height, self.wide, self.parts = height, wide, parts
        self.bands = bands
        (self.x, self.win, self.a1, self.q1, self.a2, self.u, self.t, self.a3) = scratch[:8]
        (self.s2, self.h2, self.s1, self.h1, self.c1) = scratch[8:]
        self.pairs, self.half, self.quarter = height // 2, height // 4, height // 8
        self.blocks = wide // 4

    def fill(self, load):
        x, height = self.x, self.height
        for chan in range(2):
            for h in range(height):
                x[chan, h + 1] = load(chan, h)
            x[chan, 0] = strip_above(x[chan, height], self.parts)
            x[chan, height + 1] = strip_below(x[chan, 1], self.parts)
        lane = lanes((UNITS, 128))
        count = self.wide // 8
        for t in range(self.pairs):
            pieces = [turn(x[p % 2, 2 * t + p // 2], 16 * p) for p in range(8)]
            for parity in range(2):
                group = (lane + OFF - 8 * parity + 128) // 16
                picked = pieces
                for bit in range(3):
                    take = group // (1 << bit) % 2 == 1
                    picked = [
                        jnp.where(take, picked[(i + (1 << bit)) % 8], picked[i]) for i in range(8)
                    ]
                for k in range(parity, count, 2):
                    window = turn(picked[-(k // 2) % 8], OFF - 8 * k)
                    if k == 0:
                        window = jnp.where(lane % 16 < OFF, 0.0, window)
                    if k == count - 1:
                        window = jnp.where(lane % 16 >= OFF + 8, 0.0, window)
                    self.win[t, k] = window.astype(BF16)

    def level1(self):
        lane = lanes((self.blocks, UNITS, 128))
        for t in range(self.pairs):
            values = relu(matmul([self.win[t]], self.bands[0]))
            self.a1[t] = values.astype(BF16)
            sums = [values[..., s : s + 128] + values[..., s + 128 : s + 256] for s in (0, 256)]
            both = jnp.concatenate([y[:, None] for y in sums], axis=1)
            both = both.reshape(self.blocks, UNITS, 128)
            both = both + turn(both, 64)
            side = jnp.where(lane < 96, beside(both, 1), beside(both, -1))
            self.q1[t + 1] = jnp.where(lane < 64, both, side).astype(BF16)
        self.q1[0] = strip_above(self.q1[self.pairs], self.parts).astype(BF16)
        self.q1[self.pairs + 1] = strip_below(self.q1[1], self.parts).astype(BF16)

    def level2(self):
        low = lanes((self.blocks, UNITS, 128)) < 64
        for t in range(self.half):
            values = relu(matmul([self.q1[2 * t + a] for a in range(4)], self.bands[1]))
            self.a2[t] = values.astype(BF16)
            cell = values[..., :128] + values[..., 128:]
            cell = cell + turn(cell, 64)
            self.u[t + 1] = jnp.where(low, cell, beside(cell, 1)).astype(BF16)
            left = beside(cell, -1).astype(BF16)
            if t % 2 == 0:
                self.t[t // 2, :, :, 64:] = left[..., 64:]
            else:
                self.t[(t + 1) // 2, :, :, :64] = left[..., :64]
        self.u[0] = strip_above(self.u[self.half], self.parts).astype(BF16)
        self.u[self.half + 1] = strip_below(self.u[1], self.parts).astype(BF16)
        last = self.quarter
        above = strip_above(self.t[last], self.parts).astype(BF16)
        below = strip_below(self.t[0], self.parts).astype(BF16)
        self.t[0, :, :, :64] = above[..., :64]
        self.t[last, :, :, 64:] = below[..., 64:]

    def level3(self):
        for t in range(self.quarter):
            pieces = [self.u[2 * t + a] for a in range(4)] + [self.t[t], self.t[t + 1]]
            self.a3[t + 1, 1 : self.blocks + 1] = relu(matmul(pieces, self.bands[2])).astype(BF16)
        last = self.quarter
        zero = jnp.zeros((last + 2, UNITS, 256), BF16)
        self.a3[:, 0] = zero
        self.a3[:, self.blocks + 1] = zero
        self.a3[0, :, :, 128:] = strip_above(self.a3[last, :, :, 128:], self.parts).astype(BF16)
        self.a3[last + 1, :, :, :128] = strip_below(self.a3[1, :, :, :128], self.parts).astype(BF16)

    def level3_up(self):
        count = self.blocks // 2
        low = lanes((count, UNITS, 128)) < 64
        for t in range(self.quarter):
            pieces = []
            for b in range(4):

                def column(row, start):
                    values = self.a3[row, 2 * (b // 2) : 2 * (b // 2) + self.blocks, :, start : start + 128]
                    return values.reshape(count, 2, UNITS, 128)[:, b % 2]

                pieces += [column(t, 128), column(t + 1, 0), column(t + 1, 128), column(t + 2, 0)]
            values = relu(matmul(pieces, self.bands[3]))
            for r in range(2):
                piece = values[..., 128 * r : 128 * r + 128]
                other = turn(piece, 64)
                cells = [jnp.where(low, piece, other), jnp.where(low, other, piece)]
                both = jnp.concatenate([cell[:, None] for cell in cells], axis=1)
                both = both.reshape(self.blocks, UNITS, 128)
                row = 2 * t + r
                for part in range(2):
                    span = slice(128 * part, 128 * part + 128)
                    skip = both + self.a2[row, :, :, span].astype(F32)
                    self.s2[row + 1, :, :, span] = skip.astype(BF16)
                    pairs = skip.reshape(count, 2, UNITS, 128)
                    halo = jnp.where(low, beside(pairs[:, 0], 1), beside(pairs[:, 1], -1))
                    self.h2[row + 1, :, :, span] = halo.astype(BF16)
        last = self.half
        for ref in (self.s2, self.h2):
            ref[0, :, :, 128:] = strip_above(ref[last, :, :, 128:], self.parts).astype(BF16)
            ref[last + 1, :, :, :128] = strip_below(ref[1, :, :, :128], self.parts).astype(BF16)

    def halo1(self, t, above, below):
        slot = lanes((self.blocks, UNITS, 128)) // 32
        mixed = jnp.where((slot == 0) | (slot == 3), above, turn(below, 64))
        halo = jnp.where(slot % 2 == 0, beside(mixed, 1), beside(mixed, -1))
        self.h1[t] = halo.astype(BF16)

    def level2_up(self):
        count = self.blocks // 2
        low = lanes((count, UNITS, 128)) < 64
        for t in range(self.half):
            pieces = []
            for row, start in ((t, 128), (t + 1, 0), (t + 1, 128), (t + 2, 0)):
                values = self.s2[row, :, :, start : start + 128].reshape(count, 2, UNITS, 128)
                pieces += [values[:, 0], values[:, 1], self.h2[row, :, :, start : start + 128]]
            values = relu(matmul(pieces, self.bands[4]))
            below = None
            for r in range(2):
                piece = values[..., 128 * r : 128 * r + 128]
                other = turn(piece, 64)
                cells = [jnp.where(low, piece, other), jnp.where(low, other, piece)]
                both = jnp.concatenate([cell[:, None] for cell in cells], axis=1)
                both = both.reshape(self.blocks, UNITS, 128)
                row = 2 * t + r
                skips = []
                for part in range(2):
                    parts = [
                        self.a1[row, :, :, 256 * q + 128 * part : 256 * q + 128 * part + 128][:, None]
                        for q in range(2)
                    ]
                    skip = jnp.concatenate(parts, axis=1).reshape(self.blocks, UNITS, 128)
                    skips.append(both + skip.astype(F32))
                    self.s1[row + 1, :, :, 128 * part : 128 * part + 128] = skips[part].astype(BF16)
                if r == 0 and t > 0:
                    below = self.s1[row, :, :, 128:].astype(F32)
                if row > 0:
                    self.halo1(row, below, skips[0])
                below = skips[1]
        last = self.pairs
        above = strip_above(self.s1[last, :, :, 128:], self.parts)
        self.s1[0, :, :, 128:] = above.astype(BF16)
        self.halo1(0, above, self.s1[1, :, :, :128].astype(F32))
        below = strip_below(self.s1[1, :, :, :128], self.parts)
        self.s1[last + 1, :, :, :128] = below.astype(BF16)
        self.halo1(last, self.s1[last, :, :, 128:].astype(F32), below)

    def level1_up(self, begin, end):
        s1, h1 = self.s1, self.h1
        for t in range(begin, end):
            pieces = [s1[t, :, :, 128:], s1[t + 1], s1[t + 2, :, :, :128], h1[t], h1[t + 1]]
            self.c1[t] = relu(matmul(pieces, self.bands[5])).astype(BF16)

    def last(self, begin, end, emit):
        count = self.blocks // 8
        rows = self.c1[begin:end].reshape((end - begin) * count, 8, UNITS, 256)
        values = matmul([rows[:, q] for q in range(8)], self.bands[6])
        values = values.reshape(end - begin, count, UNITS, 256)
        group = lanes((UNITS, 128)) // 32
        for t in range(begin, end):
            for half in range(2):
                span = slice(128 * half, 128 * half + 128)
                picked = [turn(values[t - begin, k, :, span], 32 * k) for k in range(4)]
                for bit in range(2):
                    take = group // (1 << bit) % 2 == 1
                    picked = [
                        jnp.where(take, picked[(i + (1 << bit)) % 4], picked[i]) for i in range(4)
                    ]
                for p in range(4 - 2 * half):
                    piece = 4 * half + p
                    emit(piece // 2, 2 * t + piece % 2, turn(picked[-p % 4], -32 * p))


def peer_id(index, inner):
    return {"slab": index // inner, "sub": lax.rem(index, inner)}


FLAT, CROSS = 13, 13


def window_kernel(peers, inner, image_ref, *refs):
    given, out_ref, bands = refs[:7], refs[7], refs[8:15]
    flat_scratch, cross_scratch = refs[15:28], refs[28:41]
    send, recv, flat, back_send, back, out_sem, in_sem, back_out_sem, back_in_sem = refs[41:50]
    plane_ref, plane, weights, local_sem = refs[50], refs[51], refs[52:59], refs[59]
    copies = [pltpu.make_async_copy(image_ref.at[:, 0], plane_ref, local_sem.at[0])]
    for number in range(7):
        copies.append(
            pltpu.make_async_copy(given[number], weights[number], local_sem.at[1 + number])
        )
    for copy in copies:
        copy.start()
    extent = plane_ref.shape[1]
    cut = extent // peers
    parts = 2 * cut
    strips = UNITS // parts
    deep = peers // strips
    tall = extent // UNITS
    me = lax.axis_index("slab") * inner + lax.axis_index("sub")

    barrier = pltpu.get_barrier_semaphore()

    def greet(k, carry):
        pl.semaphore_signal(
            barrier,
            inc=1,
            device_id=peer_id(lax.rem(me + k, peers), inner),
            device_id_type=pl.DeviceIdType.MESH,
        )
        return carry

    lax.fori_loop(1, peers, greet, 0)
    copies[0].wait()
    for chan in range(2):
        values = plane_ref[chan].astype(F32)
        plane[chan] = values
        runs = [values.reshape(peers, cut, extent), values.T.reshape(peers, cut, extent)]
        send[:, chan] = jnp.concatenate(runs, axis=1).astype(send.dtype)
    recv[pl.ds(me, 1)] = send[pl.ds(me, 1)]
    for copy in copies[1:]:
        copy.wait()
    build_all(weights, bands)
    pl.semaphore_wait(barrier, peers - 1)

    def input_copy(k):
        peer = lax.rem(me + k, peers)
        return pltpu.make_async_remote_copy(
            src_ref=send.at[peer],
            dst_ref=recv.at[me],
            send_sem=out_sem.at[k],
            recv_sem=in_sem.at[k],
            device_id=peer_id(peer, inner),
            device_id_type=pl.DeviceIdType.MESH,
        )

    def result_copy(k):
        peer = lax.rem(me + k, peers)
        return pltpu.make_async_remote_copy(
            src_ref=back_send.at[peer],
            dst_ref=back.at[me],
            send_sem=back_out_sem.at[k],
            recv_sem=back_in_sem.at[k],
            device_id=peer_id(peer, inner),
            device_id_type=pl.DeviceIdType.MESH,
        )

    def start(k, carry):
        input_copy(k).start()
        return carry

    def finish(k, carry):
        input_copy(k).wait()
        return carry

    def start_back(k, carry):
        result_copy(k).start()
        return carry

    def settle(k, carry):
        result_copy(k).wait()
        return carry

    lax.fori_loop(1, peers, start, 0)

    xy = Net(tall, extent, 1, bands, flat_scratch)
    xy.fill(lambda chan, h: plane[chan, pl.ds(h, UNITS, stride=tall), :])
    xy.level1()
    xy.level2()
    xy.level3()
    xy.level3_up()

    lax.fori_loop(1, peers, finish, 0)

    cross = Net(deep, extent, parts, bands, cross_scratch)

    def load_cross(chan, h):
        if strips == 1:
            return recv[h, chan].astype(F32)
        return recv[pl.ds(h, strips, stride=deep), chan].astype(F32).reshape(UNITS, extent)

    def emit_cross(out, h, values):
        if strips == 1:
            back_send[h, out] = values.astype(back_send.dtype)
        else:
            for strip in range(strips):
                piece = values[strip * parts : (strip + 1) * parts]
                back_send[h + strip * deep, out] = piece.astype(back_send.dtype)

    cross.fill(load_cross)
    cross.level1()
    cross.level2()
    cross.level3()
    cross.level3_up()
    cross.level2_up()
    cross.level1_up(0, cross.pairs)
    cross.last(0, cross.pairs, emit_cross)
    back[pl.ds(me, 1)] = back_send[pl.ds(me, 1)]
    lax.fori_loop(1, peers, start_back, 0)

    def emit_flat(out, h, values):
        flat[out, pl.ds(h, UNITS, stride=tall), :] = values

    xy.level2_up()
    xy.level1_up(0, xy.pairs)
    xy.last(0, xy.pairs, emit_flat)

    lax.fori_loop(1, peers, settle, 0)

    def result(run, out):
        values = back[:, out].astype(F32)[:, run * cut : (run + 1) * cut].reshape(extent, extent)
        return values.T if run == 1 else values

    out_ref[0] = (result(0, 0) + result(1, 0)) * 0.5
    out_ref[1] = (flat[0] + result(1, 1)) * 0.5
    out_ref[2] = (flat[1] + result(0, 1)) * 0.5
    out_ref[3] = (flat[2] + result(0, 2) + result(1, 2)) / 3.0


def shards(image, *weights):
    chan, _, extent, _ = image.shape
    peers = lax.axis_size(AXES)
    cut = extent // peers
    parts = 2 * cut
    link = BF16 if parts % UNITS == 0 else F32
    weights = [jnp.swapaxes(weight, 1, 2) for weight in weights[:3]] + list(weights[3:])
    sems = [pltpu.SemaphoreType.DMA((peers,))] * 4
    flows = pl.pallas_call(
        functools.partial(window_kernel, peers, lax.axis_size("sub")),
        out_shape=jax.ShapeDtypeStruct((4, extent, extent), F32),
        in_specs=[pl.BlockSpec(memory_space=pl.ANY)] * 8,
        out_specs=pl.BlockSpec(memory_space=pltpu.VMEM),
        scratch_shapes=BAND_SCRATCH
        + unit_scratch(extent // UNITS, extent)
        + unit_scratch(peers * parts // UNITS, extent)
        + [
            pltpu.VMEM((peers, chan, parts, extent), link),
            pltpu.VMEM((peers, chan, parts, extent), link),
            pltpu.VMEM((3, extent, extent), F32),
            pltpu.VMEM((peers, 3, parts, extent), link),
            pltpu.VMEM((peers, 3, parts, extent), link),
        ]
        + sems
        + [pltpu.VMEM((chan, extent, extent), BF16), pltpu.VMEM((chan, extent, extent), F32)]
        + [pltpu.VMEM(weight.shape, BF16) for weight in weights]
        + [pltpu.SemaphoreType.DMA((8,))],
        compiler_params=pltpu.CompilerParams(
            vmem_limit_bytes=62 << 20, collective_id=0, has_side_effects=True
        ),
    )(image, *weights)
    return flows[:, None]


def solution(mesh):
    split = P(None, ("groups", "slab", "sub"), None, None)
    return jax.shard_map(
        shards,
        mesh=mesh,
        in_specs=(split,) + (P(),) * 7,
        out_specs=split,
        check_vma=False,
    )
```

```python
import functools

import jax
import jax.numpy as jnp
from jax import lax
from jax.experimental import pallas as pl
from jax.experimental.pallas import tpu as pltpu
from jax.sharding import PartitionSpec as P

F32, BF16 = jnp.float32, jnp.bfloat16
AXES = ("slab", "sub")
UNITS = 16
OFF = 4
SLOTS = (0, 2, 1, 3)


def lanes(shape):
    return lax.broadcasted_iota(jnp.int32, shape, len(shape) - 1)


def turn(values, shift):
    shift = shift % 128
    return pltpu.roll(values, shift, values.ndim - 1) if shift else values


def build_band(tap, chan, made, cells, slots, scale, band_ref):
    shape = (chan, 128)
    slot_of_lane = lanes(shape) // made
    tiled = [jnp.concatenate([tap(n) * scale] * (128 // made), axis=1) for n in range(9)]
    for number, (a, b) in enumerate(cells):
        for r in range(2):
            total = jnp.zeros(shape, F32)
            for slot, c in enumerate(slots):
                down, right = a - r + 1, b - c + 1
                if 0 <= down < 3 and 0 <= right < 3:
                    value = tiled[3 * down + right]
                    total = value if len(slots) == 1 else jnp.where(slot_of_lane == slot, value, total)
            band_ref[number * chan : (number + 1) * chan, 128 * r : 128 * r + 128] = total.astype(BF16)


def build_in(tap, band_ref):
    shape = (128, 128)
    row = lax.broadcasted_iota(jnp.int32, shape, 0)
    slot = lanes(shape) // 32
    col = slot % 2 * 2 + slot // 2
    chan, down, place = row // 16 % 2, row // 32, row % 16
    tiled = [jnp.concatenate([tap(n)] * 4, axis=1) for n in range(9)]
    for q in range(2):
        right = place - OFF - 4 * q - col + 1
        ok = (right >= 0) & (right < 3)
        for r in range(2):
            code = jnp.where(ok, ((down - r) * 3 + right) * 2 + chan, -1)
            total = jnp.zeros(shape, F32)
            for number in range(9):
                for k in range(2):
                    total = jnp.where(code == number * 2 + k, tiled[number][k : k + 1, :], total)
            start = 256 * q + 128 * r
            band_ref[:, start : start + 128] = total.astype(BF16)


def build_out(weight, band_ref):
    flipped = weight.T
    shape = (32, 128)
    lane = lanes(shape)
    for q in range(8):
        for r in range(2):
            for slot, c in enumerate(SLOTS):
                start = 256 * q + 128 * r + 32 * slot
                for half in range(2):
                    total = jnp.zeros(shape, F32)
                    for out in range(3):
                        piece = 2 * out + r
                        if piece // 4 == half:
                            here = lane == 32 * (piece % 4) + 4 * q + c
                            total = jnp.where(here, flipped[:, out : out + 1], total)
                    band_ref[start : start + 32, 128 * half : 128 * half + 128] = total.astype(BF16)


CELLS_DOWN2 = [(a, b) for a in range(-1, 3) for b in (0, 1, 2, -1)]
CELLS_DOWN3 = [(a, b) for a in range(-1, 3) for b in (0, 1)] + [(a, -1) for a in range(-1, 3)]
CELLS_UP3 = [(a, b) for b in range(-1, 3) for a in range(-1, 3)]
CELLS_UP2 = [(a, b) for a in range(-1, 3) for b in (0, 1, 2, 3, 4, -1)]
CELLS_UP1 = [(a, b) for a in range(-1, 3) for b in SLOTS] + [
    (-1, 4), (0, -1), (0, 4), (-1, -1), (1, 4), (2, -1), (2, 4), (1, -1)
]


def build_all(weights, bands):
    w_in, w_down2, w_down3, w_up3, w_up2, w_up1, w_out = weights
    build_in(lambda n: w_in[n].astype(F32), bands[0])
    build_band(lambda n: w_down2[n].astype(F32), 32, 64, CELLS_DOWN2, (0, 1), 0.25, bands[1])
    build_band(lambda n: w_down3[n].astype(F32), 64, 128, CELLS_DOWN3, (0,), 0.25, bands[2])
    build_band(lambda n: w_up3[n].astype(F32).T, 128, 64, CELLS_UP3, (0, 1), 1.0, bands[3])
    build_band(lambda n: w_up2[n].astype(F32).T, 64, 32, CELLS_UP2, (0, 1, 2, 3), 1.0, bands[4])
    build_band(lambda n: w_up1[n].astype(F32).T, 32, 32, CELLS_UP1, SLOTS, 1.0, bands[5])
    build_out(w_out[...].astype(F32), bands[6])


BAND_SCRATCH = [
    pltpu.VMEM((128, 512), BF16),
    pltpu.VMEM((512, 256), BF16),
    pltpu.VMEM((768, 256), BF16),
    pltpu.VMEM((2048, 256), BF16),
    pltpu.VMEM((1536, 256), BF16),
    pltpu.VMEM((768, 256), BF16),
    pltpu.VMEM((2048, 256), BF16),
]


def beside(values, step):
    zero = jnp.zeros((1,) + values.shape[1:], values.dtype)
    if step > 0:
        return jnp.concatenate([values[1:], zero], axis=0)
    return jnp.concatenate([zero, values[:-1]], axis=0)


def strip_above(values, parts):
    values = values.astype(F32)
    if parts == UNITS:
        return jnp.zeros_like(values)
    axis = values.ndim - 2
    unit = lax.broadcasted_iota(jnp.int32, values.shape, axis)
    return jnp.where(unit < parts, 0.0, pltpu.roll(values, parts, axis))


def strip_below(values, parts):
    values = values.astype(F32)
    if parts == UNITS:
        return jnp.zeros_like(values)
    axis = values.ndim - 2
    unit = lax.broadcasted_iota(jnp.int32, values.shape, axis)
    return jnp.where(unit >= UNITS - parts, 0.0, pltpu.roll(values, UNITS - parts, axis))


def matmul(pieces, band_ref):
    rows = jnp.concatenate(pieces, axis=-1)
    lead = rows.shape[:-1]
    flat = rows.reshape(lead[0] * lead[1], rows.shape[-1])
    total = jnp.dot(flat, band_ref[...], preferred_element_type=F32)
    return total.reshape(lead + (total.shape[-1],))


def relu(values):
    return jnp.maximum(values, 0.0)


def unit_scratch(height, wide):
    pairs, half, quarter = height // 2, height // 4, height // 8
    blocks = wide // 4
    return [
        pltpu.VMEM((2, height + 2, UNITS, wide), F32),
        pltpu.VMEM((pairs, blocks // 2, UNITS, 128), BF16),
        pltpu.VMEM((pairs, blocks // 2, UNITS, 512), BF16),
        pltpu.VMEM((pairs + 2, blocks, UNITS, 128), BF16),
        pltpu.VMEM((half, blocks, UNITS, 256), BF16),
        pltpu.VMEM((half + 2, blocks, UNITS, 128), BF16),
        pltpu.VMEM((quarter + 1, blocks, UNITS, 128), BF16),
        pltpu.VMEM((quarter + 2, blocks + 2, UNITS, 256), BF16),
        pltpu.VMEM((half + 2, blocks, UNITS, 256), BF16),
        pltpu.VMEM((half + 2, blocks // 2, UNITS, 256), BF16),
        pltpu.VMEM((pairs + 2, blocks, UNITS, 256), BF16),
        pltpu.VMEM((pairs + 1, blocks, UNITS, 128), BF16),
        pltpu.VMEM((pairs, blocks, UNITS, 256), BF16),
    ]


class Net:
    def __init__(self, height, wide, parts, bands, scratch):
        self.height, self.wide, self.parts = height, wide, parts
        self.bands = bands
        (self.x, self.win, self.a1, self.q1, self.a2, self.u, self.t, self.a3) = scratch[:8]
        (self.s2, self.h2, self.s1, self.h1, self.c1) = scratch[8:]
        self.pairs, self.half, self.quarter = height // 2, height // 4, height // 8
        self.blocks = wide // 4

    def fill(self, load):
        x, height = self.x, self.height
        for chan in range(2):
            for h in range(height):
                x[chan, h + 1] = load(chan, h)
            x[chan, 0] = strip_above(x[chan, height], self.parts)
            x[chan, height + 1] = strip_below(x[chan, 1], self.parts)
        lane = lanes((UNITS, 128))
        count = self.wide // 8
        for t in range(self.pairs):
            pieces = [turn(x[p % 2, 2 * t + p // 2], 16 * p) for p in range(8)]
            for parity in range(2):
                group = (lane + OFF - 8 * parity + 128) // 16
                picked = pieces
                for bit in range(3):
                    take = group // (1 << bit) % 2 == 1
                    picked = [
                        jnp.where(take, picked[(i + (1 << bit)) % 8], picked[i]) for i in range(8)
                    ]
                for k in range(parity, count, 2):
                    window = turn(picked[-(k // 2) % 8], OFF - 8 * k)
                    if k == 0:
                        window = jnp.where(lane % 16 < OFF, 0.0, window)
                    if k == count - 1:
                        window = jnp.where(lane % 16 >= OFF + 8, 0.0, window)
                    self.win[t, k] = window.astype(BF16)

    def level1(self):
        lane = lanes((self.blocks, UNITS, 128))
        for t in range(self.pairs):
            values = relu(matmul([self.win[t]], self.bands[0]))
            self.a1[t] = values.astype(BF16)
            sums = [values[..., s : s + 128] + values[..., s + 128 : s + 256] for s in (0, 256)]
            both = jnp.concatenate([y[:, None] for y in sums], axis=1)
            both = both.reshape(self.blocks, UNITS, 128)
            both = both + turn(both, 64)
            side = jnp.where(lane < 96, beside(both, 1), beside(both, -1))
            self.q1[t + 1] = jnp.where(lane < 64, both, side).astype(BF16)
        self.q1[0] = strip_above(self.q1[self.pairs], self.parts).astype(BF16)
        self.q1[self.pairs + 1] = strip_below(self.q1[1], self.parts).astype(BF16)

    def level2(self):
        low = lanes((self.blocks, UNITS, 128)) < 64
        for t in range(self.half):
            values = relu(matmul([self.q1[2 * t + a] for a in range(4)], self.bands[1]))
            self.a2[t] = values.astype(BF16)
            cell = values[..., :128] + values[..., 128:]
            cell = cell + turn(cell, 64)
            self.u[t + 1] = jnp.where(low, cell, beside(cell, 1)).astype(BF16)
            left = beside(cell, -1).astype(BF16)
            if t % 2 == 0:
                self.t[t // 2, :, :, 64:] = left[..., 64:]
            else:
                self.t[(t + 1) // 2, :, :, :64] = left[..., :64]
        self.u[0] = strip_above(self.u[self.half], self.parts).astype(BF16)
        self.u[self.half + 1] = strip_below(self.u[1], self.parts).astype(BF16)
        last = self.quarter
        above = strip_above(self.t[last], self.parts).astype(BF16)
        below = strip_below(self.t[0], self.parts).astype(BF16)
        self.t[0, :, :, :64] = above[..., :64]
        self.t[last, :, :, 64:] = below[..., 64:]

    def level3(self):
        for t in range(self.quarter):
            pieces = [self.u[2 * t + a] for a in range(4)] + [self.t[t], self.t[t + 1]]
            self.a3[t + 1, 1 : self.blocks + 1] = relu(matmul(pieces, self.bands[2])).astype(BF16)
        last = self.quarter
        zero = jnp.zeros((last + 2, UNITS, 256), BF16)
        self.a3[:, 0] = zero
        self.a3[:, self.blocks + 1] = zero
        self.a3[0, :, :, 128:] = strip_above(self.a3[last, :, :, 128:], self.parts).astype(BF16)
        self.a3[last + 1, :, :, :128] = strip_below(self.a3[1, :, :, :128], self.parts).astype(BF16)

    def level3_up(self):
        count = self.blocks // 2
        low = lanes((count, UNITS, 128)) < 64
        for t in range(self.quarter):
            pieces = []
            for b in range(4):

                def column(row, start):
                    values = self.a3[row, 2 * (b // 2) : 2 * (b // 2) + self.blocks, :, start : start + 128]
                    return values.reshape(count, 2, UNITS, 128)[:, b % 2]

                pieces += [column(t, 128), column(t + 1, 0), column(t + 1, 128), column(t + 2, 0)]
            values = relu(matmul(pieces, self.bands[3]))
            for r in range(2):
                piece = values[..., 128 * r : 128 * r + 128]
                other = turn(piece, 64)
                cells = [jnp.where(low, piece, other), jnp.where(low, other, piece)]
                both = jnp.concatenate([cell[:, None] for cell in cells], axis=1)
                both = both.reshape(self.blocks, UNITS, 128)
                row = 2 * t + r
                for part in range(2):
                    span = slice(128 * part, 128 * part + 128)
                    skip = both + self.a2[row, :, :, span].astype(F32)
                    self.s2[row + 1, :, :, span] = skip.astype(BF16)
                    pairs = skip.reshape(count, 2, UNITS, 128)
                    halo = jnp.where(low, beside(pairs[:, 0], 1), beside(pairs[:, 1], -1))
                    self.h2[row + 1, :, :, span] = halo.astype(BF16)
        last = self.half
        for ref in (self.s2, self.h2):
            ref[0, :, :, 128:] = strip_above(ref[last, :, :, 128:], self.parts).astype(BF16)
            ref[last + 1, :, :, :128] = strip_below(ref[1, :, :, :128], self.parts).astype(BF16)

    def halo1(self, t, above, below):
        slot = lanes((self.blocks, UNITS, 128)) // 32
        mixed = jnp.where((slot == 0) | (slot == 3), above, turn(below, 64))
        halo = jnp.where(slot % 2 == 0, beside(mixed, 1), beside(mixed, -1))
        self.h1[t] = halo.astype(BF16)

    def level2_up(self):
        count = self.blocks // 2
        low = lanes((count, UNITS, 128)) < 64
        for t in range(self.half):
            pieces = []
            for row, start in ((t, 128), (t + 1, 0), (t + 1, 128), (t + 2, 0)):
                values = self.s2[row, :, :, start : start + 128].reshape(count, 2, UNITS, 128)
                pieces += [values[:, 0], values[:, 1], self.h2[row, :, :, start : start + 128]]
            values = relu(matmul(pieces, self.bands[4]))
            below = None
            for r in range(2):
                piece = values[..., 128 * r : 128 * r + 128]
                other = turn(piece, 64)
                cells = [jnp.where(low, piece, other), jnp.where(low, other, piece)]
                both = jnp.concatenate([cell[:, None] for cell in cells], axis=1)
                both = both.reshape(self.blocks, UNITS, 128)
                row = 2 * t + r
                skips = []
                for part in range(2):
                    parts = [
                        self.a1[row, :, :, 256 * q + 128 * part : 256 * q + 128 * part + 128][:, None]
                        for q in range(2)
                    ]
                    skip = jnp.concatenate(parts, axis=1).reshape(self.blocks, UNITS, 128)
                    skips.append(both + skip.astype(F32))
                    self.s1[row + 1, :, :, 128 * part : 128 * part + 128] = skips[part].astype(BF16)
                if r == 0 and t > 0:
                    below = self.s1[row, :, :, 128:].astype(F32)
                if row > 0:
                    self.halo1(row, below, skips[0])
                below = skips[1]
        last = self.pairs
        above = strip_above(self.s1[last, :, :, 128:], self.parts)
        self.s1[0, :, :, 128:] = above.astype(BF16)
        self.halo1(0, above, self.s1[1, :, :, :128].astype(F32))
        below = strip_below(self.s1[1, :, :, :128], self.parts)
        self.s1[last + 1, :, :, :128] = below.astype(BF16)
        self.halo1(last, self.s1[last, :, :, 128:].astype(F32), below)

    def level1_up(self, begin, end):
        s1, h1 = self.s1, self.h1
        for t in range(begin, end):
            pieces = [s1[t, :, :, 128:], s1[t + 1], s1[t + 2, :, :, :128], h1[t], h1[t + 1]]
            self.c1[t] = relu(matmul(pieces, self.bands[5])).astype(BF16)

    def last(self, begin, end, emit):
        count = self.blocks // 8
        rows = self.c1[begin:end].reshape((end - begin) * count, 8, UNITS, 256)
        values = matmul([rows[:, q] for q in range(8)], self.bands[6])
        values = values.reshape(end - begin, count, UNITS, 256)
        group = lanes((UNITS, 128)) // 32
        for t in range(begin, end):
            for half in range(2):
                span = slice(128 * half, 128 * half + 128)
                picked = [turn(values[t - begin, k, :, span], 32 * k) for k in range(4)]
                for bit in range(2):
                    take = group // (1 << bit) % 2 == 1
                    picked = [
                        jnp.where(take, picked[(i + (1 << bit)) % 4], picked[i]) for i in range(4)
                    ]
                for p in range(4 - 2 * half):
                    piece = 4 * half + p
                    emit(piece // 2, 2 * t + piece % 2, turn(picked[-p % 4], -32 * p))


def peer_id(index, inner):
    return {"slab": index // inner, "sub": lax.rem(index, inner)}


FLAT, CROSS = 13, 13


def window_kernel(peers, inner, image_ref, *refs):
    given, out_ref, bands = refs[:7], refs[7], refs[8:15]
    flat_scratch, cross_scratch = refs[15:28], refs[28:41]
    send, recv, flat, back_send, back, out_sem, in_sem, back_out_sem, back_in_sem = refs[41:50]
    plane_ref, plane, weights, local_sem = refs[50], refs[51], refs[52:59], refs[59]
    copies = [pltpu.make_async_copy(image_ref.at[:, 0], plane_ref, local_sem.at[0])]
    for number in range(7):
        copies.append(
            pltpu.make_async_copy(given[number], weights[number], local_sem.at[1 + number])
        )
    for copy in copies:
        copy.start()
    extent = plane_ref.shape[1]
    cut = extent // peers
    parts = 2 * cut
    strips = UNITS // parts
    deep = peers // strips
    tall = extent // UNITS
    me = lax.axis_index("slab") * inner + lax.axis_index("sub")

    barrier = pltpu.get_barrier_semaphore()

    def greet(k, carry):
        pl.semaphore_signal(
            barrier,
            inc=1,
            device_id=peer_id(lax.rem(me + k, peers), inner),
            device_id_type=pl.DeviceIdType.MESH,
        )
        return carry

    lax.fori_loop(1, peers, greet, 0)
    copies[0].wait()
    for chan in range(2):
        values = plane_ref[chan].astype(F32)
        plane[chan] = values
        runs = [values.reshape(peers, cut, extent), values.T.reshape(peers, cut, extent)]
        send[:, chan] = jnp.concatenate(runs, axis=1).astype(send.dtype)
    recv[pl.ds(me, 1)] = send[pl.ds(me, 1)]
    for copy in copies[1:]:
        copy.wait()
    build_all(weights, bands)
    pl.semaphore_wait(barrier, peers - 1)

    def input_copy(k):
        peer = lax.rem(me + k, peers)
        return pltpu.make_async_remote_copy(
            src_ref=send.at[peer],
            dst_ref=recv.at[me],
            send_sem=out_sem.at[k],
            recv_sem=in_sem.at[k],
            device_id=peer_id(peer, inner),
            device_id_type=pl.DeviceIdType.MESH,
        )

    def result_copy(k):
        peer = lax.rem(me + k, peers)
        return pltpu.make_async_remote_copy(
            src_ref=back_send.at[peer],
            dst_ref=back.at[me],
            send_sem=back_out_sem.at[k],
            recv_sem=back_in_sem.at[k],
            device_id=peer_id(peer, inner),
            device_id_type=pl.DeviceIdType.MESH,
        )

    def start(k, carry):
        input_copy(k).start()
        return carry

    def finish(k, carry):
        input_copy(k).wait()
        return carry

    def start_back(k, carry):
        result_copy(k).start()
        return carry

    def settle(k, carry):
        result_copy(k).wait()
        return carry

    lax.fori_loop(1, peers, start, 0)

    xy = Net(tall, extent, 1, bands, flat_scratch)
    xy.fill(lambda chan, h: plane[chan, pl.ds(h, UNITS, stride=tall), :])
    xy.level1()
    xy.level2()
    xy.level3()
    xy.level3_up()

    lax.fori_loop(1, peers, finish, 0)

    cross = Net(deep, extent, parts, bands, cross_scratch)

    def load_cross(chan, h):
        if strips == 1:
            return recv[h, chan].astype(F32)
        return recv[pl.ds(h, strips, stride=deep), chan].astype(F32).reshape(UNITS, extent)

    def emit_cross(out, h, values):
        if strips == 1:
            back_send[h, out] = values.astype(back_send.dtype)
        else:
            for strip in range(strips):
                piece = values[strip * parts : (strip + 1) * parts]
                back_send[h + strip * deep, out] = piece.astype(back_send.dtype)

    cross.fill(load_cross)
    cross.level1()
    cross.level2()
    cross.level3()
    cross.level3_up()
    cross.level2_up()
    cross.level1_up(0, cross.pairs)
    cross.last(0, cross.pairs, emit_cross)
    back[pl.ds(me, 1)] = back_send[pl.ds(me, 1)]
    lax.fori_loop(1, peers, start_back, 0)

    def emit_flat(out, h, values):
        flat[out, pl.ds(h, UNITS, stride=tall), :] = values

    xy.level2_up()
    xy.level1_up(0, xy.pairs)
    xy.last(0, xy.pairs, emit_flat)

    lax.fori_loop(1, peers, settle, 0)

    def result(run, out):
        values = back[:, out].astype(F32)[:, run * cut : (run + 1) * cut].reshape(extent, extent)
        return values.T if run == 1 else values

    out_ref[0] = (result(0, 0) + result(1, 0)) * 0.5
    out_ref[1] = (flat[0] + result(1, 1)) * 0.5
    out_ref[2] = (flat[1] + result(0, 1)) * 0.5
    out_ref[3] = (flat[2] + result(0, 2) + result(1, 2)) / 3.0


def shards(image, *weights):
    chan, _, extent, _ = image.shape
    peers = lax.axis_size(AXES)
    cut = extent // peers
    parts = 2 * cut
    link = BF16 if parts % UNITS == 0 else F32
    weights = [jnp.swapaxes(weight, 1, 2) for weight in weights[:3]] + list(weights[3:])
    image, *weights = [pltpu.with_memory_space_constraint(x, pltpu.HBM) for x in (image, *weights)]
    sems = [pltpu.SemaphoreType.DMA((peers,))] * 4
    flows = pl.pallas_call(
        functools.partial(window_kernel, peers, lax.axis_size("sub")),
        out_shape=jax.ShapeDtypeStruct((4, extent, extent), F32),
        in_specs=[pl.BlockSpec(memory_space=pltpu.HBM)] * 8,
        out_specs=pl.BlockSpec(memory_space=pltpu.VMEM),
        scratch_shapes=BAND_SCRATCH
        + unit_scratch(extent // UNITS, extent)
        + unit_scratch(peers * parts // UNITS, extent)
        + [
            pltpu.VMEM((peers, chan, parts, extent), link),
            pltpu.VMEM((peers, chan, parts, extent), link),
            pltpu.VMEM((3, extent, extent), F32),
            pltpu.VMEM((peers, 3, parts, extent), link),
            pltpu.VMEM((peers, 3, parts, extent), link),
        ]
        + sems
        + [pltpu.VMEM((chan, extent, extent), BF16), pltpu.VMEM((chan, extent, extent), F32)]
        + [pltpu.VMEM(weight.shape, BF16) for weight in weights]
        + [pltpu.SemaphoreType.DMA((8,))],
        compiler_params=pltpu.CompilerParams(
            vmem_limit_bytes=50 << 20, collective_id=0, has_side_effects=True
        ),
    )(image, *weights)
    return flows[:, None]


def solution(mesh):
    split = P(None, ("groups", "slab", "sub"), None, None)
    return jax.shard_map(
        shards,
        mesh=mesh,
        in_specs=(split,) + (P(),) * 7,
        out_specs=split,
        check_vma=False,
    )
```

```python
import functools

import jax
import jax.numpy as jnp
from jax import lax
from jax.experimental import pallas as pl
from jax.experimental.pallas import tpu as pltpu
from jax.sharding import PartitionSpec as P

F32, BF16 = jnp.float32, jnp.bfloat16
AXES = ("slab", "sub")
UNITS = 16
OFF = 4
SLOTS = (0, 2, 1, 3)


def lanes(shape):
    return lax.broadcasted_iota(jnp.int32, shape, len(shape) - 1)


def turn(values, shift):
    shift = shift % 128
    return pltpu.roll(values, shift, values.ndim - 1) if shift else values


def build_band(tap, chan, made, cells, slots, scale, band_ref):
    shape = (chan, 128)
    slot_of_lane = lanes(shape) // made
    tiled = [jnp.concatenate([tap(n) * scale] * (128 // made), axis=1) for n in range(9)]
    for number, (a, b) in enumerate(cells):
        for r in range(2):
            total = jnp.zeros(shape, F32)
            for slot, c in enumerate(slots):
                down, right = a - r + 1, b - c + 1
                if 0 <= down < 3 and 0 <= right < 3:
                    value = tiled[3 * down + right]
                    total = value if len(slots) == 1 else jnp.where(slot_of_lane == slot, value, total)
            band_ref[number * chan : (number + 1) * chan, 128 * r : 128 * r + 128] = total.astype(BF16)


def build_in(tap, band_ref):
    shape = (128, 128)
    row = lax.broadcasted_iota(jnp.int32, shape, 0)
    slot = lanes(shape) // 32
    col = slot % 2 * 2 + slot // 2
    chan, down, place = row // 16 % 2, row // 32, row % 16
    tiled = [jnp.concatenate([tap(n)] * 4, axis=1) for n in range(9)]
    for q in range(2):
        right = place - OFF - 4 * q - col + 1
        ok = (right >= 0) & (right < 3)
        for r in range(2):
            code = jnp.where(ok, ((down - r) * 3 + right) * 2 + chan, -1)
            total = jnp.zeros(shape, F32)
            for number in range(9):
                for k in range(2):
                    total = jnp.where(code == number * 2 + k, tiled[number][k : k + 1, :], total)
            start = 256 * q + 128 * r
            band_ref[:, start : start + 128] = total.astype(BF16)


def build_out(weight, band_ref):
    flipped = weight.T
    shape = (32, 128)
    lane = lanes(shape)
    for q in range(8):
        for r in range(2):
            for slot, c in enumerate(SLOTS):
                start = 256 * q + 128 * r + 32 * slot
                for half in range(2):
                    total = jnp.zeros(shape, F32)
                    for out in range(3):
                        piece = 2 * out + r
                        if piece // 4 == half:
                            here = lane == 32 * (piece % 4) + 4 * q + c
                            total = jnp.where(here, flipped[:, out : out + 1], total)
                    band_ref[start : start + 32, 128 * half : 128 * half + 128] = total.astype(BF16)


CELLS_DOWN2 = [(a, b) for a in range(-1, 3) for b in (0, 1, 2, -1)]
CELLS_DOWN3 = [(a, b) for a in range(-1, 3) for b in (0, 1)] + [(a, -1) for a in range(-1, 3)]
CELLS_UP3 = [(a, b) for b in range(-1, 3) for a in range(-1, 3)]
CELLS_UP2 = [(a, b) for a in range(-1, 3) for b in (0, 1, 2, 3, 4, -1)]
CELLS_UP1 = [(a, b) for a in range(-1, 3) for b in SLOTS] + [
    (-1, 4), (0, -1), (0, 4), (-1, -1), (1, 4), (2, -1), (2, 4), (1, -1)
]


def build_all(weights, bands):
    w_in, w_down2, w_down3, w_up3, w_up2, w_up1, w_out = weights
    build_in(lambda n: w_in[n].astype(F32), bands[0])
    build_band(lambda n: w_down2[n].astype(F32), 32, 64, CELLS_DOWN2, (0, 1), 0.25, bands[1])
    build_band(lambda n: w_down3[n].astype(F32), 64, 128, CELLS_DOWN3, (0,), 0.25, bands[2])
    build_band(lambda n: w_up3[n].astype(F32).T, 128, 64, CELLS_UP3, (0, 1), 1.0, bands[3])
    build_band(lambda n: w_up2[n].astype(F32).T, 64, 32, CELLS_UP2, (0, 1, 2, 3), 1.0, bands[4])
    build_band(lambda n: w_up1[n].astype(F32).T, 32, 32, CELLS_UP1, SLOTS, 1.0, bands[5])
    build_out(w_out[...].astype(F32), bands[6])


BAND_SCRATCH = [
    pltpu.VMEM((128, 512), BF16),
    pltpu.VMEM((512, 256), BF16),
    pltpu.VMEM((768, 256), BF16),
    pltpu.VMEM((2048, 256), BF16),
    pltpu.VMEM((1536, 256), BF16),
    pltpu.VMEM((768, 256), BF16),
    pltpu.VMEM((2048, 256), BF16),
]


def beside(values, step):
    zero = jnp.zeros((1,) + values.shape[1:], values.dtype)
    if step > 0:
        return jnp.concatenate([values[1:], zero], axis=0)
    return jnp.concatenate([zero, values[:-1]], axis=0)


def strip_above(values, parts):
    values = values.astype(F32)
    if parts == UNITS:
        return jnp.zeros_like(values)
    axis = values.ndim - 2
    unit = lax.broadcasted_iota(jnp.int32, values.shape, axis)
    return jnp.where(unit < parts, 0.0, pltpu.roll(values, parts, axis))


def strip_below(values, parts):
    values = values.astype(F32)
    if parts == UNITS:
        return jnp.zeros_like(values)
    axis = values.ndim - 2
    unit = lax.broadcasted_iota(jnp.int32, values.shape, axis)
    return jnp.where(unit >= UNITS - parts, 0.0, pltpu.roll(values, UNITS - parts, axis))


def matmul(pieces, band_ref):
    rows = jnp.concatenate(pieces, axis=-1)
    lead = rows.shape[:-1]
    flat = rows.reshape(lead[0] * lead[1], rows.shape[-1])
    total = jnp.dot(flat, band_ref[...], preferred_element_type=F32)
    return total.reshape(lead + (total.shape[-1],))


def relu(values):
    return jnp.maximum(values, 0.0)


def unit_scratch(height, wide):
    pairs, half, quarter = height // 2, height // 4, height // 8
    blocks = wide // 4
    return [
        pltpu.VMEM((2, height + 2, UNITS, wide), F32),
        pltpu.VMEM((pairs, blocks // 2, UNITS, 128), BF16),
        pltpu.VMEM((pairs, blocks // 2, UNITS, 512), BF16),
        pltpu.VMEM((pairs + 2, blocks, UNITS, 128), BF16),
        pltpu.VMEM((half, blocks, UNITS, 256), BF16),
        pltpu.VMEM((half + 2, blocks, UNITS, 128), BF16),
        pltpu.VMEM((quarter + 1, blocks, UNITS, 128), BF16),
        pltpu.VMEM((quarter + 2, blocks + 2, UNITS, 256), BF16),
        pltpu.VMEM((half + 2, blocks, UNITS, 256), BF16),
        pltpu.VMEM((half + 2, blocks // 2, UNITS, 256), BF16),
        pltpu.VMEM((pairs + 2, blocks, UNITS, 256), BF16),
        pltpu.VMEM((pairs + 1, blocks, UNITS, 128), BF16),
        pltpu.VMEM((pairs, blocks, UNITS, 256), BF16),
    ]


class Net:
    def __init__(self, height, wide, parts, bands, scratch):
        self.height, self.wide, self.parts = height, wide, parts
        self.bands = bands
        (self.x, self.win, self.a1, self.q1, self.a2, self.u, self.t, self.a3) = scratch[:8]
        (self.s2, self.h2, self.s1, self.h1, self.c1) = scratch[8:]
        self.pairs, self.half, self.quarter = height // 2, height // 4, height // 8
        self.blocks = wide // 4

    def fill(self, load):
        x, height = self.x, self.height
        for chan in range(2):
            for h in range(height):
                x[chan, h + 1] = load(chan, h)
            x[chan, 0] = strip_above(x[chan, height], self.parts)
            x[chan, height + 1] = strip_below(x[chan, 1], self.parts)
        lane = lanes((UNITS, 128))
        count = self.wide // 8
        for t in range(self.pairs):
            pieces = [turn(x[p % 2, 2 * t + p // 2], 16 * p) for p in range(8)]
            for parity in range(2):
                group = (lane + OFF - 8 * parity + 128) // 16
                picked = pieces
                for bit in range(3):
                    take = group // (1 << bit) % 2 == 1
                    picked = [
                        jnp.where(take, picked[(i + (1 << bit)) % 8], picked[i]) for i in range(8)
                    ]
                for k in range(parity, count, 2):
                    window = turn(picked[-(k // 2) % 8], OFF - 8 * k)
                    if k == 0:
                        window = jnp.where(lane % 16 < OFF, 0.0, window)
                    if k == count - 1:
                        window = jnp.where(lane % 16 >= OFF + 8, 0.0, window)
                    self.win[t, k] = window.astype(BF16)

    def level1(self):
        lane = lanes((self.blocks, UNITS, 128))
        for t in range(self.pairs):
            values = relu(matmul([self.win[t]], self.bands[0]))
            self.a1[t] = values.astype(BF16)
            sums = [values[..., s : s + 128] + values[..., s + 128 : s + 256] for s in (0, 256)]
            both = jnp.concatenate([y[:, None] for y in sums], axis=1)
            both = both.reshape(self.blocks, UNITS, 128)
            both = both + turn(both, 64)
            side = jnp.where(lane < 96, beside(both, 1), beside(both, -1))
            self.q1[t + 1] = jnp.where(lane < 64, both, side).astype(BF16)
        self.q1[0] = strip_above(self.q1[self.pairs], self.parts).astype(BF16)
        self.q1[self.pairs + 1] = strip_below(self.q1[1], self.parts).astype(BF16)

    def level2(self):
        low = lanes((self.blocks, UNITS, 128)) < 64
        for t in range(self.half):
            values = relu(matmul([self.q1[2 * t + a] for a in range(4)], self.bands[1]))
            self.a2[t] = values.astype(BF16)
            cell = values[..., :128] + values[..., 128:]
            cell = cell + turn(cell, 64)
            self.u[t + 1] = jnp.where(low, cell, beside(cell, 1)).astype(BF16)
            left = beside(cell, -1).astype(BF16)
            if t % 2 == 0:
                self.t[t // 2, :, :, 64:] = left[..., 64:]
            else:
                self.t[(t + 1) // 2, :, :, :64] = left[..., :64]
        self.u[0] = strip_above(self.u[self.half], self.parts).astype(BF16)
        self.u[self.half + 1] = strip_below(self.u[1], self.parts).astype(BF16)
        last = self.quarter
        above = strip_above(self.t[last], self.parts).astype(BF16)
        below = strip_below(self.t[0], self.parts).astype(BF16)
        self.t[0, :, :, :64] = above[..., :64]
        self.t[last, :, :, 64:] = below[..., 64:]

    def level3(self):
        for t in range(self.quarter):
            pieces = [self.u[2 * t + a] for a in range(4)] + [self.t[t], self.t[t + 1]]
            self.a3[t + 1, 1 : self.blocks + 1] = relu(matmul(pieces, self.bands[2])).astype(BF16)
        last = self.quarter
        zero = jnp.zeros((last + 2, UNITS, 256), BF16)
        self.a3[:, 0] = zero
        self.a3[:, self.blocks + 1] = zero
        self.a3[0, :, :, 128:] = strip_above(self.a3[last, :, :, 128:], self.parts).astype(BF16)
        self.a3[last + 1, :, :, :128] = strip_below(self.a3[1, :, :, :128], self.parts).astype(BF16)

    def level3_up(self):
        count = self.blocks // 2
        low = lanes((count, UNITS, 128)) < 64
        for t in range(self.quarter):
            pieces = []
            for b in range(4):

                def column(row, start):
                    values = self.a3[row, 2 * (b // 2) : 2 * (b // 2) + self.blocks, :, start : start + 128]
                    return values.reshape(count, 2, UNITS, 128)[:, b % 2]

                pieces += [column(t, 128), column(t + 1, 0), column(t + 1, 128), column(t + 2, 0)]
            values = relu(matmul(pieces, self.bands[3]))
            for r in range(2):
                piece = values[..., 128 * r : 128 * r + 128]
                other = turn(piece, 64)
                cells = [jnp.where(low, piece, other), jnp.where(low, other, piece)]
                both = jnp.concatenate([cell[:, None] for cell in cells], axis=1)
                both = both.reshape(self.blocks, UNITS, 128)
                row = 2 * t + r
                for part in range(2):
                    span = slice(128 * part, 128 * part + 128)
                    skip = both + self.a2[row, :, :, span].astype(F32)
                    self.s2[row + 1, :, :, span] = skip.astype(BF16)
                    pairs = skip.reshape(count, 2, UNITS, 128)
                    halo = jnp.where(low, beside(pairs[:, 0], 1), beside(pairs[:, 1], -1))
                    self.h2[row + 1, :, :, span] = halo.astype(BF16)
        last = self.half
        for ref in (self.s2, self.h2):
            ref[0, :, :, 128:] = strip_above(ref[last, :, :, 128:], self.parts).astype(BF16)
            ref[last + 1, :, :, :128] = strip_below(ref[1, :, :, :128], self.parts).astype(BF16)

    def halo1(self, t, above, below):
        slot = lanes((self.blocks, UNITS, 128)) // 32
        mixed = jnp.where((slot == 0) | (slot == 3), above, turn(below, 64))
        halo = jnp.where(slot % 2 == 0, beside(mixed, 1), beside(mixed, -1))
        self.h1[t] = halo.astype(BF16)

    def level2_up(self):
        count = self.blocks // 2
        low = lanes((count, UNITS, 128)) < 64
        for t in range(self.half):
            pieces = []
            for row, start in ((t, 128), (t + 1, 0), (t + 1, 128), (t + 2, 0)):
                values = self.s2[row, :, :, start : start + 128].reshape(count, 2, UNITS, 128)
                pieces += [values[:, 0], values[:, 1], self.h2[row, :, :, start : start + 128]]
            values = relu(matmul(pieces, self.bands[4]))
            below = None
            for r in range(2):
                piece = values[..., 128 * r : 128 * r + 128]
                other = turn(piece, 64)
                cells = [jnp.where(low, piece, other), jnp.where(low, other, piece)]
                both = jnp.concatenate([cell[:, None] for cell in cells], axis=1)
                both = both.reshape(self.blocks, UNITS, 128)
                row = 2 * t + r
                skips = []
                for part in range(2):
                    parts = [
                        self.a1[row, :, :, 256 * q + 128 * part : 256 * q + 128 * part + 128][:, None]
                        for q in range(2)
                    ]
                    skip = jnp.concatenate(parts, axis=1).reshape(self.blocks, UNITS, 128)
                    skips.append(both + skip.astype(F32))
                    self.s1[row + 1, :, :, 128 * part : 128 * part + 128] = skips[part].astype(BF16)
                if r == 0 and t > 0:
                    below = self.s1[row, :, :, 128:].astype(F32)
                if row > 0:
                    self.halo1(row, below, skips[0])
                below = skips[1]
        last = self.pairs
        above = strip_above(self.s1[last, :, :, 128:], self.parts)
        self.s1[0, :, :, 128:] = above.astype(BF16)
        self.halo1(0, above, self.s1[1, :, :, :128].astype(F32))
        below = strip_below(self.s1[1, :, :, :128], self.parts)
        self.s1[last + 1, :, :, :128] = below.astype(BF16)
        self.halo1(last, self.s1[last, :, :, 128:].astype(F32), below)

    def level1_up(self, begin, end):
        s1, h1 = self.s1, self.h1
        for t in range(begin, end):
            pieces = [s1[t, :, :, 128:], s1[t + 1], s1[t + 2, :, :, :128], h1[t], h1[t + 1]]
            self.c1[t] = relu(matmul(pieces, self.bands[5])).astype(BF16)

    def last(self, begin, end, emit):
        count = self.blocks // 8
        rows = self.c1[begin:end].reshape((end - begin) * count, 8, UNITS, 256)
        values = matmul([rows[:, q] for q in range(8)], self.bands[6])
        values = values.reshape(end - begin, count, UNITS, 256)
        group = lanes((UNITS, 128)) // 32
        for t in range(begin, end):
            for half in range(2):
                span = slice(128 * half, 128 * half + 128)
                picked = [turn(values[t - begin, k, :, span], 32 * k) for k in range(4)]
                for bit in range(2):
                    take = group // (1 << bit) % 2 == 1
                    picked = [
                        jnp.where(take, picked[(i + (1 << bit)) % 4], picked[i]) for i in range(4)
                    ]
                for p in range(4 - 2 * half):
                    piece = 4 * half + p
                    emit(piece // 2, 2 * t + piece % 2, turn(picked[-p % 4], -32 * p))


def peer_id(index, inner):
    return {"slab": index // inner, "sub": lax.rem(index, inner)}


GROUP = 2


def window_kernel(peers, inner, image_ref, *refs):
    given, out_ref, bands = refs[:7], refs[7], refs[8:15]
    flat_scratch, cross_scratch = refs[15:28], refs[28:41]
    send, recv, flat, back_send, back, out_sem, in_sem, back_out_sem, back_in_sem = refs[41:50]
    plane_ref, plane, weights, local_sem = refs[50], refs[51], refs[52:59], refs[59]
    copies = [pltpu.make_async_copy(image_ref.at[:, 0], plane_ref, local_sem.at[0])]
    for number in range(7):
        copies.append(
            pltpu.make_async_copy(given[number], weights[number], local_sem.at[1 + number])
        )
    copies[0].start()
    extent = plane_ref.shape[1]
    cut = extent // peers
    parts = 2 * cut
    strips = UNITS // parts
    deep = peers // strips
    tall = extent // UNITS
    me = lax.axis_index("slab") * inner + lax.axis_index("sub")

    barrier = pltpu.get_barrier_semaphore()

    def greet(k, carry):
        pl.semaphore_signal(
            barrier,
            inc=1,
            device_id=peer_id(lax.rem(me + k, peers), inner),
            device_id_type=pl.DeviceIdType.MESH,
        )
        return carry

    lax.fori_loop(1, peers, greet, 0)
    for copy in copies[1:]:
        copy.start()
    copies[0].wait()
    for chan in range(2):
        values = plane_ref[chan].astype(F32)
        plane[chan] = values
        runs = [values.reshape(peers, cut, extent), values.T.reshape(peers, cut, extent)]
        send[:, chan] = jnp.concatenate(runs, axis=1).astype(send.dtype)
    recv[pl.ds(me, 1)] = send[pl.ds(me, 1)]
    for copy in copies[1:]:
        copy.wait()
    build_all(weights, bands)
    pl.semaphore_wait(barrier, peers - 1)

    def input_copy(k):
        peer = lax.rem(me + k, peers)
        return pltpu.make_async_remote_copy(
            src_ref=send.at[peer],
            dst_ref=recv.at[me],
            send_sem=out_sem.at[k],
            recv_sem=in_sem.at[k],
            device_id=peer_id(peer, inner),
            device_id_type=pl.DeviceIdType.MESH,
        )

    def result_copy(k):
        peer = lax.rem(me + k, peers)
        return pltpu.make_async_remote_copy(
            src_ref=back_send.at[peer],
            dst_ref=back.at[me],
            send_sem=back_out_sem.at[k],
            recv_sem=back_in_sem.at[k],
            device_id=peer_id(peer, inner),
            device_id_type=pl.DeviceIdType.MESH,
        )

    def start(k, carry):
        input_copy(k).start()
        return carry

    def finish(k, carry):
        input_copy(k).wait()
        return carry

    def start_back(k, carry):
        result_copy(k).start()
        return carry

    def settle(k, carry):
        result_copy(k).wait()
        return carry

    lax.fori_loop(1, peers, start, 0)

    xy = Net(tall, extent, 1, bands, flat_scratch)
    xy.fill(lambda chan, h: plane[chan, pl.ds(h, UNITS, stride=tall), :])
    xy.level1()
    xy.level2()
    xy.level3()
    xy.level3_up()

    lax.fori_loop(1, peers, finish, 0)

    cross = Net(deep, extent, parts, bands, cross_scratch)

    def load_cross(chan, h):
        if strips == 1:
            return recv[h, chan].astype(F32)
        return recv[pl.ds(h, strips, stride=deep), chan].astype(F32).reshape(UNITS, extent)

    def emit_cross(out, h, values):
        if strips == 1:
            back_send[h, out] = values.astype(back_send.dtype)
        else:
            for strip in range(strips):
                piece = values[strip * parts : (strip + 1) * parts]
                back_send[h + strip * deep, out] = piece.astype(back_send.dtype)

    cross.fill(load_cross)
    cross.level1()
    cross.level2()
    cross.level3()
    cross.level3_up()
    cross.level2_up()
    for begin in range(0, cross.pairs, GROUP):
        cross.level1_up(begin, begin + GROUP)
        cross.last(begin, begin + GROUP, emit_cross)
        if strips == 1:

            def start_ready(k, carry):
                peer = 2 * begin + k

                @pl.when(peer != me)
                def _():
                    result_copy(lax.rem(peer + peers - me, peers)).start()

                return carry

            lax.fori_loop(0, 2 * GROUP, start_ready, 0)
    back[pl.ds(me, 1)] = back_send[pl.ds(me, 1)]
    if strips > 1:
        lax.fori_loop(1, peers, start_back, 0)

    def emit_flat(out, h, values):
        flat[out, pl.ds(h, UNITS, stride=tall), :] = values

    xy.level2_up()
    xy.level1_up(0, xy.pairs)
    xy.last(0, xy.pairs, emit_flat)

    lax.fori_loop(1, peers, settle, 0)

    def result(run, out):
        values = back[:, out].astype(F32)[:, run * cut : (run + 1) * cut].reshape(extent, extent)
        return values.T if run == 1 else values

    out_ref[0] = (result(0, 0) + result(1, 0)) * 0.5
    out_ref[1] = (flat[0] + result(1, 1)) * 0.5
    out_ref[2] = (flat[1] + result(0, 1)) * 0.5
    out_ref[3] = (flat[2] + result(0, 2) + result(1, 2)) / 3.0


def shards(image, *weights):
    chan, _, extent, _ = image.shape
    peers = lax.axis_size(AXES)
    cut = extent // peers
    parts = 2 * cut
    link = BF16 if parts % UNITS == 0 else F32
    weights = [jnp.swapaxes(weight, 1, 2) for weight in weights[:3]] + list(weights[3:])
    image, *weights = [pltpu.with_memory_space_constraint(x, pltpu.HBM) for x in (image, *weights)]
    sems = [pltpu.SemaphoreType.DMA((peers,))] * 4
    flows = pl.pallas_call(
        functools.partial(window_kernel, peers, lax.axis_size("sub")),
        out_shape=jax.ShapeDtypeStruct((4, extent, extent), F32),
        in_specs=[pl.BlockSpec(memory_space=pltpu.HBM)] * 8,
        out_specs=pl.BlockSpec(memory_space=pltpu.VMEM),
        scratch_shapes=BAND_SCRATCH
        + unit_scratch(extent // UNITS, extent)
        + unit_scratch(peers * parts // UNITS, extent)
        + [
            pltpu.VMEM((peers, chan, parts, extent), link),
            pltpu.VMEM((peers, chan, parts, extent), link),
            pltpu.VMEM((3, extent, extent), F32),
            pltpu.VMEM((peers, 3, parts, extent), link),
            pltpu.VMEM((peers, 3, parts, extent), link),
        ]
        + sems
        + [pltpu.VMEM((chan, extent, extent), BF16), pltpu.VMEM((chan, extent, extent), F32)]
        + [pltpu.VMEM(weight.shape, BF16) for weight in weights]
        + [pltpu.SemaphoreType.DMA((8,))],
        compiler_params=pltpu.CompilerParams(
            vmem_limit_bytes=50 << 20, collective_id=0, has_side_effects=True
        ),
    )(image, *weights)
    return flows[:, None]


def solution(mesh):
    split = P(None, ("groups", "slab", "sub"), None, None)
    return jax.shard_map(
        shards,
        mesh=mesh,
        in_specs=(split,) + (P(),) * 7,
        out_specs=split,
        check_vma=False,
    )
```

```python
import functools

import jax
import jax.numpy as jnp
from jax import lax
from jax.experimental import pallas as pl
from jax.experimental.pallas import tpu as pltpu
from jax.sharding import PartitionSpec as P

F32, BF16 = jnp.float32, jnp.bfloat16
AXES = ("slab", "sub")
UNITS = 16
OFF = 4
SLOTS = (0, 2, 1, 3)


def lanes(shape):
    return lax.broadcasted_iota(jnp.int32, shape, len(shape) - 1)


def turn(values, shift):
    shift = shift % 128
    return pltpu.roll(values, shift, values.ndim - 1) if shift else values


def build_band(tap, chan, made, cells, slots, scale, band_ref):
    shape = (chan, 128)
    slot_of_lane = lanes(shape) // made
    tiled = [jnp.concatenate([tap(n) * scale] * (128 // made), axis=1) for n in range(9)]
    for number, (a, b) in enumerate(cells):
        for r in range(2):
            total = jnp.zeros(shape, F32)
            for slot, c in enumerate(slots):
                down, right = a - r + 1, b - c + 1
                if 0 <= down < 3 and 0 <= right < 3:
                    value = tiled[3 * down + right]
                    total = value if len(slots) == 1 else jnp.where(slot_of_lane == slot, value, total)
            band_ref[number * chan : (number + 1) * chan, 128 * r : 128 * r + 128] = total.astype(BF16)


def build_in(tap, band_ref):
    shape = (128, 128)
    row = lax.broadcasted_iota(jnp.int32, shape, 0)
    slot = lanes(shape) // 32
    col = slot % 2 * 2 + slot // 2
    chan, down, place = row // 16 % 2, row // 32, row % 16
    tiled = [jnp.concatenate([tap(n)] * 4, axis=1) for n in range(9)]
    for q in range(2):
        right = place - OFF - 4 * q - col + 1
        ok = (right >= 0) & (right < 3)
        for r in range(2):
            code = jnp.where(ok, ((down - r) * 3 + right) * 2 + chan, -1)
            total = jnp.zeros(shape, F32)
            for number in range(9):
                for k in range(2):
                    total = jnp.where(code == number * 2 + k, tiled[number][k : k + 1, :], total)
            start = 256 * q + 128 * r
            band_ref[:, start : start + 128] = total.astype(BF16)


def build_out(weight, band_ref):
    flipped = weight.T
    shape = (32, 128)
    lane = lanes(shape)
    for q in range(8):
        for r in range(2):
            for slot, c in enumerate(SLOTS):
                start = 256 * q + 128 * r + 32 * slot
                for half in range(2):
                    total = jnp.zeros(shape, F32)
                    for out in range(3):
                        piece = 2 * out + r
                        if piece // 4 == half:
                            here = lane == 32 * (piece % 4) + 4 * q + c
                            total = jnp.where(here, flipped[:, out : out + 1], total)
                    band_ref[start : start + 32, 128 * half : 128 * half + 128] = total.astype(BF16)


CELLS_DOWN2 = [(a, b) for a in range(-1, 3) for b in (0, 1, 2, -1)]
CELLS_DOWN3 = [(a, b) for a in range(-1, 3) for b in (0, 1)] + [(a, -1) for a in range(-1, 3)]
CELLS_UP3 = [(a, b) for b in range(-1, 3) for a in range(-1, 3)]
CELLS_UP2 = [(a, b) for a in range(-1, 3) for b in (0, 1, 2, 3, 4, -1)]
CELLS_UP1 = [(a, b) for a in range(-1, 3) for b in SLOTS] + [
    (-1, 4), (0, -1), (0, 4), (-1, -1), (1, 4), (2, -1), (2, 4), (1, -1)
]


def build_all(weights, bands):
    w_in, w_down2, w_down3, w_up3, w_up2, w_up1, w_out = weights
    build_in(lambda n: w_in[n].astype(F32), bands[0])
    build_band(lambda n: w_down2[n].astype(F32), 32, 64, CELLS_DOWN2, (0, 1), 0.25, bands[1])
    build_band(lambda n: w_down3[n].astype(F32), 64, 128, CELLS_DOWN3, (0,), 0.25, bands[2])
    build_band(lambda n: w_up3[n].astype(F32).T, 128, 64, CELLS_UP3, (0, 1), 1.0, bands[3])
    build_band(lambda n: w_up2[n].astype(F32).T, 64, 32, CELLS_UP2, (0, 1, 2, 3), 1.0, bands[4])
    build_band(lambda n: w_up1[n].astype(F32).T, 32, 32, CELLS_UP1, SLOTS, 1.0, bands[5])
    build_out(w_out[...].astype(F32), bands[6])


BAND_SCRATCH = [
    pltpu.VMEM((128, 512), BF16),
    pltpu.VMEM((512, 256), BF16),
    pltpu.VMEM((768, 256), BF16),
    pltpu.VMEM((2048, 256), BF16),
    pltpu.VMEM((1536, 256), BF16),
    pltpu.VMEM((768, 256), BF16),
    pltpu.VMEM((2048, 256), BF16),
]


def beside(values, step):
    zero = jnp.zeros((1,) + values.shape[1:], values.dtype)
    if step > 0:
        return jnp.concatenate([values[1:], zero], axis=0)
    return jnp.concatenate([zero, values[:-1]], axis=0)


def strip_above(values, parts):
    values = values.astype(F32)
    if parts == UNITS:
        return jnp.zeros_like(values)
    axis = values.ndim - 2
    unit = lax.broadcasted_iota(jnp.int32, values.shape, axis)
    return jnp.where(unit < parts, 0.0, pltpu.roll(values, parts, axis))


def strip_below(values, parts):
    values = values.astype(F32)
    if parts == UNITS:
        return jnp.zeros_like(values)
    axis = values.ndim - 2
    unit = lax.broadcasted_iota(jnp.int32, values.shape, axis)
    return jnp.where(unit >= UNITS - parts, 0.0, pltpu.roll(values, UNITS - parts, axis))


def matmul(pieces, band_ref):
    rows = jnp.concatenate(pieces, axis=-1)
    lead = rows.shape[:-1]
    flat = rows.reshape(lead[0] * lead[1], rows.shape[-1])
    total = jnp.dot(flat, band_ref[...], preferred_element_type=F32)
    return total.reshape(lead + (total.shape[-1],))


def relu(values):
    return jnp.maximum(values, 0.0)


def unit_scratch(height, wide):
    pairs, half, quarter = height // 2, height // 4, height // 8
    blocks = wide // 4
    return [
        pltpu.VMEM((2, height + 2, UNITS, wide), F32),
        pltpu.VMEM((pairs, blocks // 2, UNITS, 128), BF16),
        pltpu.VMEM((pairs, blocks // 2, UNITS, 512), BF16),
        pltpu.VMEM((pairs + 2, blocks, UNITS, 128), BF16),
        pltpu.VMEM((half, blocks, UNITS, 256), BF16),
        pltpu.VMEM((half + 2, blocks, UNITS, 128), BF16),
        pltpu.VMEM((quarter + 1, blocks, UNITS, 128), BF16),
        pltpu.VMEM((quarter + 2, blocks + 2, UNITS, 256), BF16),
        pltpu.VMEM((half + 2, blocks, UNITS, 256), BF16),
        pltpu.VMEM((half + 2, blocks // 2, UNITS, 256), BF16),
        pltpu.VMEM((pairs + 2, blocks, UNITS, 256), BF16),
        pltpu.VMEM((pairs + 1, blocks, UNITS, 128), BF16),
        pltpu.VMEM((pairs, blocks, UNITS, 256), BF16),
    ]


class Net:
    def __init__(self, height, wide, parts, bands, scratch):
        self.height, self.wide, self.parts = height, wide, parts
        self.bands = bands
        (self.x, self.win, self.a1, self.q1, self.a2, self.u, self.t, self.a3) = scratch[:8]
        (self.s2, self.h2, self.s1, self.h1, self.c1) = scratch[8:]
        self.pairs, self.half, self.quarter = height // 2, height // 4, height // 8
        self.blocks = wide // 4

    def fill(self, load):
        x, height = self.x, self.height
        for chan in range(2):
            for h in range(height):
                x[chan, h + 1] = load(chan, h)
            x[chan, 0] = strip_above(x[chan, height], self.parts)
            x[chan, height + 1] = strip_below(x[chan, 1], self.parts)
        lane = lanes((UNITS, 128))
        count = self.wide // 8
        for t in range(self.pairs):
            pieces = [turn(x[p % 2, 2 * t + p // 2], 16 * p) for p in range(8)]
            for parity in range(2):
                group = (lane + OFF - 8 * parity + 128) // 16
                picked = pieces
                for bit in range(3):
                    take = group // (1 << bit) % 2 == 1
                    picked = [
                        jnp.where(take, picked[(i + (1 << bit)) % 8], picked[i]) for i in range(8)
                    ]
                for k in range(parity, count, 2):
                    window = turn(picked[-(k // 2) % 8], OFF - 8 * k)
                    if k == 0:
                        window = jnp.where(lane % 16 < OFF, 0.0, window)
                    if k == count - 1:
                        window = jnp.where(lane % 16 >= OFF + 8, 0.0, window)
                    self.win[t, k] = window.astype(BF16)

    def level1(self):
        lane = lanes((self.blocks, UNITS, 128))
        for t in range(self.pairs):
            values = relu(matmul([self.win[t]], self.bands[0]))
            self.a1[t] = values.astype(BF16)
            sums = [values[..., s : s + 128] + values[..., s + 128 : s + 256] for s in (0, 256)]
            both = jnp.concatenate([y[:, None] for y in sums], axis=1)
            both = both.reshape(self.blocks, UNITS, 128)
            both = both + turn(both, 64)
            side = jnp.where(lane < 96, beside(both, 1), beside(both, -1))
            self.q1[t + 1] = jnp.where(lane < 64, both, side).astype(BF16)
        self.q1[0] = strip_above(self.q1[self.pairs], self.parts).astype(BF16)
        self.q1[self.pairs + 1] = strip_below(self.q1[1], self.parts).astype(BF16)

    def level2(self):
        low = lanes((self.blocks, UNITS, 128)) < 64
        for t in range(self.half):
            values = relu(matmul([self.q1[2 * t + a] for a in range(4)], self.bands[1]))
            self.a2[t] = values.astype(BF16)
            cell = values[..., :128] + values[..., 128:]
            cell = cell + turn(cell, 64)
            self.u[t + 1] = jnp.where(low, cell, beside(cell, 1)).astype(BF16)
            left = beside(cell, -1).astype(BF16)
            if t % 2 == 0:
                self.t[t // 2, :, :, 64:] = left[..., 64:]
            else:
                self.t[(t + 1) // 2, :, :, :64] = left[..., :64]
        self.u[0] = strip_above(self.u[self.half], self.parts).astype(BF16)
        self.u[self.half + 1] = strip_below(self.u[1], self.parts).astype(BF16)
        last = self.quarter
        above = strip_above(self.t[last], self.parts).astype(BF16)
        below = strip_below(self.t[0], self.parts).astype(BF16)
        self.t[0, :, :, :64] = above[..., :64]
        self.t[last, :, :, 64:] = below[..., 64:]

    def level3(self):
        for t in range(self.quarter):
            pieces = [self.u[2 * t + a] for a in range(4)] + [self.t[t], self.t[t + 1]]
            self.a3[t + 1, 1 : self.blocks + 1] = relu(matmul(pieces, self.bands[2])).astype(BF16)
        last = self.quarter
        zero = jnp.zeros((last + 2, UNITS, 256), BF16)
        self.a3[:, 0] = zero
        self.a3[:, self.blocks + 1] = zero
        self.a3[0, :, :, 128:] = strip_above(self.a3[last, :, :, 128:], self.parts).astype(BF16)
        self.a3[last + 1, :, :, :128] = strip_below(self.a3[1, :, :, :128], self.parts).astype(BF16)

    def level3_up(self):
        count = self.blocks // 2
        low = lanes((count, UNITS, 128)) < 64
        for t in range(self.quarter):
            pieces = []
            for b in range(4):

                def column(row, start):
                    values = self.a3[row, 2 * (b // 2) : 2 * (b // 2) + self.blocks, :, start : start + 128]
                    return values.reshape(count, 2, UNITS, 128)[:, b % 2]

                pieces += [column(t, 128), column(t + 1, 0), column(t + 1, 128), column(t + 2, 0)]
            values = relu(matmul(pieces, self.bands[3]))
            for r in range(2):
                piece = values[..., 128 * r : 128 * r + 128]
                other = turn(piece, 64)
                cells = [jnp.where(low, piece, other), jnp.where(low, other, piece)]
                both = jnp.concatenate([cell[:, None] for cell in cells], axis=1)
                both = both.reshape(self.blocks, UNITS, 128)
                row = 2 * t + r
                for part in range(2):
                    span = slice(128 * part, 128 * part + 128)
                    skip = both + self.a2[row, :, :, span].astype(F32)
                    self.s2[row + 1, :, :, span] = skip.astype(BF16)
                    pairs = skip.reshape(count, 2, UNITS, 128)
                    halo = jnp.where(low, beside(pairs[:, 0], 1), beside(pairs[:, 1], -1))
                    self.h2[row + 1, :, :, span] = halo.astype(BF16)
        last = self.half
        for ref in (self.s2, self.h2):
            ref[0, :, :, 128:] = strip_above(ref[last, :, :, 128:], self.parts).astype(BF16)
            ref[last + 1, :, :, :128] = strip_below(ref[1, :, :, :128], self.parts).astype(BF16)

    def halo1(self, t, above, below):
        slot = lanes((self.blocks, UNITS, 128)) // 32
        mixed = jnp.where((slot == 0) | (slot == 3), above, turn(below, 64))
        halo = jnp.where(slot % 2 == 0, beside(mixed, 1), beside(mixed, -1))
        self.h1[t] = halo.astype(BF16)

    def level2_up(self):
        count = self.blocks // 2
        low = lanes((count, UNITS, 128)) < 64
        for t in range(self.half):
            pieces = []
            for row, start in ((t, 128), (t + 1, 0), (t + 1, 128), (t + 2, 0)):
                values = self.s2[row, :, :, start : start + 128].reshape(count, 2, UNITS, 128)
                pieces += [values[:, 0], values[:, 1], self.h2[row, :, :, start : start + 128]]
            values = relu(matmul(pieces, self.bands[4]))
            below = None
            for r in range(2):
                piece = values[..., 128 * r : 128 * r + 128]
                other = turn(piece, 64)
                cells = [jnp.where(low, piece, other), jnp.where(low, other, piece)]
                both = jnp.concatenate([cell[:, None] for cell in cells], axis=1)
                both = both.reshape(self.blocks, UNITS, 128)
                row = 2 * t + r
                skips = []
                for part in range(2):
                    parts = [
                        self.a1[row, :, :, 256 * q + 128 * part : 256 * q + 128 * part + 128][:, None]
                        for q in range(2)
                    ]
                    skip = jnp.concatenate(parts, axis=1).reshape(self.blocks, UNITS, 128)
                    skips.append(both + skip.astype(F32))
                    self.s1[row + 1, :, :, 128 * part : 128 * part + 128] = skips[part].astype(BF16)
                if r == 0 and t > 0:
                    below = self.s1[row, :, :, 128:].astype(F32)
                if row > 0:
                    self.halo1(row, below, skips[0])
                below = skips[1]
        last = self.pairs
        above = strip_above(self.s1[last, :, :, 128:], self.parts)
        self.s1[0, :, :, 128:] = above.astype(BF16)
        self.halo1(0, above, self.s1[1, :, :, :128].astype(F32))
        below = strip_below(self.s1[1, :, :, :128], self.parts)
        self.s1[last + 1, :, :, :128] = below.astype(BF16)
        self.halo1(last, self.s1[last, :, :, 128:].astype(F32), below)

    def level1_up(self, begin, end):
        s1, h1 = self.s1, self.h1
        for t in range(begin, end):
            pieces = [s1[t, :, :, 128:], s1[t + 1], s1[t + 2, :, :, :128], h1[t], h1[t + 1]]
            self.c1[t] = relu(matmul(pieces, self.bands[5])).astype(BF16)

    def last(self, begin, end, emit):
        count = self.blocks // 8
        rows = self.c1[begin:end].reshape((end - begin) * count, 8, UNITS, 256)
        values = matmul([rows[:, q] for q in range(8)], self.bands[6])
        values = values.reshape(end - begin, count, UNITS, 256)
        group = lanes((UNITS, 128)) // 32
        for t in range(begin, end):
            for half in range(2):
                span = slice(128 * half, 128 * half + 128)
                picked = [turn(values[t - begin, k, :, span], 32 * k) for k in range(4)]
                for bit in range(2):
                    take = group // (1 << bit) % 2 == 1
                    picked = [
                        jnp.where(take, picked[(i + (1 << bit)) % 4], picked[i]) for i in range(4)
                    ]
                for p in range(4 - 2 * half):
                    piece = 4 * half + p
                    emit(piece // 2, 2 * t + piece % 2, turn(picked[-p % 4], -32 * p))


def peer_id(index, inner):
    return {"slab": index // inner, "sub": lax.rem(index, inner)}


GROUP = 2


def window_kernel(peers, inner, image_ref, *refs):
    given, out_ref, bands = refs[:7], refs[7], refs[8:15]
    flat_scratch, cross_scratch = refs[15:28], refs[28:41]
    send, recv, flat, back_send, back, out_sem, in_sem, back_out_sem, back_in_sem = refs[41:50]
    plane_ref, plane, weights, local_sem = refs[50], refs[51], refs[52:59], refs[59]
    copies = [pltpu.make_async_copy(image_ref.at[:, 0], plane_ref, local_sem.at[0])]
    for number in range(7):
        copies.append(
            pltpu.make_async_copy(given[number], weights[number], local_sem.at[1 + number])
        )
    copies[0].start()
    extent = plane_ref.shape[1]
    cut = extent // peers
    parts = 2 * cut
    strips = UNITS // parts
    deep = peers // strips
    tall = extent // UNITS
    me = lax.axis_index("slab") * inner + lax.axis_index("sub")

    barrier = pltpu.get_barrier_semaphore()

    def greet(k, carry):
        pl.semaphore_signal(
            barrier,
            inc=1,
            device_id=peer_id(lax.rem(me + k, peers), inner),
            device_id_type=pl.DeviceIdType.MESH,
        )
        return carry

    lax.fori_loop(1, peers, greet, 0)
    for copy in copies[1:]:
        copy.start()
    copies[0].wait()
    for chan in range(2):
        values = plane_ref[chan].astype(F32)
        plane[chan] = values
        runs = [values.reshape(peers, cut, extent), values.T.reshape(peers, cut, extent)]
        send[:, chan] = jnp.concatenate(runs, axis=1).astype(send.dtype)
    recv[pl.ds(me, 1)] = send[pl.ds(me, 1)]
    for copy in copies[1:]:
        copy.wait()
    build_all(weights, bands)
    pl.semaphore_wait(barrier, peers - 1)

    def input_copy(k):
        peer = lax.rem(me + k, peers)
        return pltpu.make_async_remote_copy(
            src_ref=send.at[peer],
            dst_ref=recv.at[me],
            send_sem=out_sem.at[k],
            recv_sem=in_sem.at[k],
            device_id=peer_id(peer, inner),
            device_id_type=pl.DeviceIdType.MESH,
        )

    def result_copy(k):
        peer = lax.rem(me + k, peers)
        return pltpu.make_async_remote_copy(
            src_ref=back_send.at[peer],
            dst_ref=back.at[me],
            send_sem=back_out_sem.at[k],
            recv_sem=back_in_sem.at[k],
            device_id=peer_id(peer, inner),
            device_id_type=pl.DeviceIdType.MESH,
        )

    def start(k, carry):
        input_copy(k).start()
        return carry

    def finish(k, carry):
        input_copy(k).wait()
        return carry

    def start_back(k, carry):
        result_copy(k).start()
        return carry

    def settle(k, carry):
        result_copy(k).wait()
        return carry

    def start_asc(k, carry):
        @pl.when(k != me)
        def _():
            input_copy(lax.rem(k + peers - me, peers)).start()

        return carry

    lax.fori_loop(0, peers, start_asc, 0)

    xy = Net(tall, extent, 1, bands, flat_scratch)
    xy.fill(lambda chan, h: plane[chan, pl.ds(h, UNITS, stride=tall), :])
    xy.level1()
    xy.level2()
    xy.level3()
    xy.level3_up()
    xy.level2_up()
    xy.level1_up(0, xy.pairs)

    lax.fori_loop(1, peers, finish, 0)

    cross = Net(deep, extent, parts, bands, cross_scratch)

    def load_cross(chan, h):
        if strips == 1:
            return recv[h, chan].astype(F32)
        return recv[pl.ds(h, strips, stride=deep), chan].astype(F32).reshape(UNITS, extent)

    def emit_cross(out, h, values):
        if strips == 1:
            back_send[h, out] = values.astype(back_send.dtype)
        else:
            for strip in range(strips):
                piece = values[strip * parts : (strip + 1) * parts]
                back_send[h + strip * deep, out] = piece.astype(back_send.dtype)

    cross.fill(load_cross)
    cross.level1()
    cross.level2()
    cross.level3()
    cross.level3_up()
    cross.level2_up()
    for begin in range(0, cross.pairs, GROUP):
        cross.level1_up(begin, begin + GROUP)
        cross.last(begin, begin + GROUP, emit_cross)
        if strips == 1:

            def start_ready(k, carry):
                peer = 2 * begin + k

                @pl.when(peer != me)
                def _():
                    result_copy(lax.rem(peer + peers - me, peers)).start()

                return carry

            lax.fori_loop(0, 2 * GROUP, start_ready, 0)
    back[pl.ds(me, 1)] = back_send[pl.ds(me, 1)]
    if strips > 1:
        lax.fori_loop(1, peers, start_back, 0)

    def emit_flat(out, h, values):
        flat[out, pl.ds(h, UNITS, stride=tall), :] = values

    xy.last(0, xy.pairs, emit_flat)

    lax.fori_loop(1, peers, settle, 0)

    def result(run, out):
        values = back[:, out].astype(F32)[:, run * cut : (run + 1) * cut].reshape(extent, extent)
        return values.T if run == 1 else values

    out_ref[0] = (result(0, 0) + result(1, 0)) * 0.5
    out_ref[1] = (flat[0] + result(1, 1)) * 0.5
    out_ref[2] = (flat[1] + result(0, 1)) * 0.5
    out_ref[3] = (flat[2] + result(0, 2) + result(1, 2)) / 3.0


def shards(image, *weights):
    chan, _, extent, _ = image.shape
    peers = lax.axis_size(AXES)
    cut = extent // peers
    parts = 2 * cut
    link = BF16 if parts % UNITS == 0 else F32
    weights = [jnp.swapaxes(weight, 1, 2) for weight in weights[:3]] + list(weights[3:])
    image, *weights = [pltpu.with_memory_space_constraint(x, pltpu.HBM) for x in (image, *weights)]
    sems = [pltpu.SemaphoreType.DMA((peers,))] * 4
    flows = pl.pallas_call(
        functools.partial(window_kernel, peers, lax.axis_size("sub")),
        out_shape=jax.ShapeDtypeStruct((4, extent, extent), F32),
        in_specs=[pl.BlockSpec(memory_space=pltpu.HBM)] * 8,
        out_specs=pl.BlockSpec(memory_space=pltpu.VMEM),
        scratch_shapes=BAND_SCRATCH
        + unit_scratch(extent // UNITS, extent)
        + unit_scratch(peers * parts // UNITS, extent)
        + [
            pltpu.VMEM((peers, chan, parts, extent), link),
            pltpu.VMEM((peers, chan, parts, extent), link),
            pltpu.VMEM((3, extent, extent), F32),
            pltpu.VMEM((peers, 3, parts, extent), link),
            pltpu.VMEM((peers, 3, parts, extent), link),
        ]
        + sems
        + [pltpu.VMEM((chan, extent, extent), BF16), pltpu.VMEM((chan, extent, extent), F32)]
        + [pltpu.VMEM(weight.shape, BF16) for weight in weights]
        + [pltpu.SemaphoreType.DMA((8,))],
        compiler_params=pltpu.CompilerParams(
            vmem_limit_bytes=50 << 20, collective_id=0, has_side_effects=True
        ),
    )(image, *weights)
    return flows[:, None]


def solution(mesh):
    split = P(None, ("groups", "slab", "sub"), None, None)
    return jax.shard_map(
        shards,
        mesh=mesh,
        in_specs=(split,) + (P(),) * 7,
        out_specs=split,
        check_vma=False,
    )
```
